32 devices in a mesh: grid: 8 (over y, x, core), ipts: 4 (over z).
Axes of the slice: x: 2, y: 2, z: 4, core: 2. Of those that a mesh axis runs over, the one named last changes fastest.
Arguments:
- orbitals: bfloat16 [16384, 1024], P(('grid', 'ipts')), may hold values from -1.1953125 to 1.1953125
- targets: bfloat16 [16384, 256], P(('grid', 'ipts')), may hold values from -6 to 6
- points: int32 [4, 1024], P('ipts', 'grid'), may hold values from 0 to 16383, as said below
- potential: bfloat16 [16384, 4096], P('grid', 'ipts'), may hold values from -0.09375 to 0.09375
Outputs:
- exchanged: bfloat16 [16384, 256], P(('grid', 'ipts'))
The draws below stay inside these ranges and needn't reach their ends.
Inputs may be any that keep to these rules, and one draw needn't show every extreme that they name: Indices are distinct over all groups; each row of points rises strictly, and its entries k * 128 to (k + 1) * 128 - 1 lie in grid rows k * 2048 to (k + 1) * 2048 - 1.
All inputs are finite; a program needn't handle non-finite values.
Results may differ from the reference program's by a relative error of at most 0.0049.
Values may be sent and summed in bfloat16 or wider, within the bound.
A program may use at most 128 MiB of HBM per device.

```python
import jax
import jax.numpy as jnp
from jax import lax

NORB = 1024
NJ = 256
PTS_SLAB = 128
SLAB = 2048
GROUPS = 4
PER_GROUP = 1024
NG = 16384
NMU = 4096


def draw_points(key, part):
    slabs = PER_GROUP // PTS_SLAB
    keys = jax.random.split(jax.random.fold_in(key, 7), slabs)

    def one_slab(slab_key):
        order = jax.random.permutation(slab_key, SLAB)
        chosen = order[:GROUPS * PTS_SLAB].reshape(GROUPS, PTS_SLAB)
        return jnp.sort(chosen, axis=1).astype(jnp.int32)
    picks = jax.vmap(one_slab)(keys)
    offsets = (jnp.arange(slabs, dtype=jnp.int32) * SLAB)[:, None, None]
    return jnp.transpose(picks + offsets, (1, 0, 2)).reshape(GROUPS, PER_GROUP)


def steps_of(own_key, extent, cuts, low, top_value):
    gain = 1.0
    for position, parts in cuts:
        draws = jax.random.uniform(jax.random.fold_in(jax.random.fold_in(own_key, 6), position), (parts,), jnp.float32, low / len(cuts), top_value / len(cuts))
        gain = gain * jnp.repeat(jnp.exp(draws), extent[position] // parts).reshape((-1,) + (1,) * (len(extent) - 1 - position))
    return gain


def scatter_about(key, extent, deviation, bound, cuts=(), kind=jnp.bfloat16):
    factor_of = steps_of(key, extent, cuts, -0.22, 0.18) if cuts else 1.0
    values = jax.random.normal(key, extent, jnp.float32) * deviation * factor_of
    return jnp.minimum(jnp.maximum(values, -bound), bound).astype(kind)


def setup_inputs(seed: int = 0) -> dict:
    splits = jax.random.split(jax.random.key(seed), 5)
    orbitals = scatter_about(splits[0], (NG, NORB), 0.2, 1.1953125, ((0, 32),))
    targets = scatter_about(splits[1], (NG, NJ), 1.0, 6.0, ((0, 32),))
    points = draw_points(jax.random.fold_in(splits[4], 71), 0)
    potential = scatter_about(splits[3], (NG, NMU), (4 * PER_GROUP) ** -0.5, 0.09375, ((0, 8), (1, 4)))
    return dict(orbitals=orbitals, targets=targets, points=points, potential=potential)


def reference(orbitals, targets, points, potential):
    slabs = NG // SLAB
    values = []
    for group in range(GROUPS):
        index = points[group]
        values.append((jnp.take(orbitals, index, axis=0), jnp.take(targets, index, axis=0)))

    def one_slab(slab_index):
        start = slab_index * SLAB
        rows = lax.dynamic_slice_in_dim(orbitals, start, SLAB, 0)
        kernel_rows = lax.dynamic_slice_in_dim(potential, start, SLAB, 0)
        total = jnp.zeros((SLAB, NJ), jnp.float32)
        for group in range(GROUPS):
            orbital_values, target_values = values[group]
            products = lax.dot_general(rows, orbital_values, (((1,), (1,)), ((), ())), preferred_element_type=jnp.float32)
            kernel = kernel_rows[:, group * PER_GROUP:(group + 1) * PER_GROUP].astype(jnp.float32)
            weighted = (kernel * products).astype(jnp.bfloat16)
            total = total + jnp.dot(weighted, target_values, preferred_element_type=jnp.float32)
        return (-total).astype(jnp.bfloat16)

    result = lax.map(one_slab, jnp.arange(slabs, dtype=jnp.int32))
    return result.reshape(NG, NJ)
```

```python
import functools

import jax
import jax.numpy as jnp
from jax import lax
from jax.experimental import pallas as pl
from jax.experimental.pallas import tpu as pltpu
from jax.sharding import PartitionSpec as P

MESH = pl.DeviceIdType.MESH
LANES = 128
WIDTH = 1024
SPLIT = 2
EARLY = 4
F32, BF16 = jnp.float32, jnp.bfloat16


class Names:
    def __init__(self, size):
        self.size, self.known = size, {}

    def __getitem__(self, name):
        number = self.known.setdefault(name, len(self.known))
        assert number < self.size
        return number


def kernel(groups, slabs, orbitals, targets, points, potential, out,
           slab, values, target_values, weights, lent, target_rows, index, hot, far_hot,
           early_out, early_near, early_in, leaving, arriving, crossing, kept, kept_end,
           local_sem, send_sem, recv_sem, plane_send, plane_recv):
    g = lax.axis_index("grid")
    z = lax.axis_index("ipts")
    side = z // 2
    q = z + side * (groups - 1 - 2 * z)
    inward, outward = z + 1 - 2 * side, z - 1 + 2 * side
    rows, norb = orbitals.shape
    nj = targets.shape[1]
    count = points.shape[1]
    total = slabs * count
    lanes = slabs // 2
    partner = g + 1 - 2 * lax.rem(g, 2)
    early = norb // EARLY
    tail = norb - early
    pieces = tail // LANES
    sub = rows // SPLIT
    width = min(WIDTH, total)
    names = Names(send_sem.shape[0])
    sent = []

    def where(block):
        return block + side * (groups - 1 - 2 * block)

    def cols(k):
        return pl.ds(k * LANES, LANES)

    last = pl.ds(tail, early)

    def place(slab_index):
        return pl.ds(pl.multiple_of(slab_index * count, count), count)

    def peer(step):
        return lax.rem(g + 2 * step, slabs)

    def source(base, step):
        return lax.rem(base + slabs - 2 * step, slabs)

    def send(name, src, dst, target):
        copy = pltpu.make_async_remote_copy(
            src_ref=src, dst_ref=dst, send_sem=send_sem.at[names[name]], recv_sem=recv_sem.at[names[name]],
            device_id={"grid": g, "ipts": target}, device_id_type=MESH)
        copy.start()
        sent.append(copy)

    def receive(name, dst):
        pltpu.make_async_remote_copy(
            src_ref=dst, dst_ref=dst, send_sem=send_sem.at[names[name]], recv_sem=recv_sem.at[names[name]],
            device_id={"grid": g, "ipts": z}, device_id_type=MESH).wait_recv()

    def across(ref, item, way, target):
        return pltpu.make_async_remote_copy(
            src_ref=ref, dst_ref=ref, send_sem=plane_send.at[item, way], recv_sem=plane_recv.at[item, way],
            device_id={"grid": target, "ipts": z}, device_id_type=MESH)

    def spread(item, view):
        for step in range(1, lanes):
            copy = across(view(place(g)), item, step, peer(step))
            copy.start()
            sent.append(copy)
        copy = across(view(place(g)), item, 0, partner)
        copy.start()
        sent.append(copy)

    def forward(item, view):
        for step in range(1, lanes):
            block = view(place(source(g, step)))
            across(block, item, step, g).wait_recv()
            copy = across(block, item, lanes + step, partner)
            copy.start()
            sent.append(copy)

    def gathered(item, view):
        across(view(place(partner)), item, 0, g).wait_recv()
        for step in range(1, lanes):
            across(view(place(source(partner, step))), item, lanes + step, g).wait_recv()

    def contribution(block, half, slot, kernel_rows):
        part = pl.ds(half * sub, sub)
        acc = None
        for start in range(0, total, width):
            some = pl.ds(start, width)
            products = lax.dot_general(
                slab[block, part, :], values[slot, some, :], (((1,), (1,)), ((), ())),
                preferred_element_type=F32)
            weighted = (kernel_rows[part, some].astype(F32) * products).astype(BF16)
            term = jnp.dot(weighted, target_values[slot, some, :], preferred_element_type=F32)
            acc = term if acc is None else acc + term
        return acc

    own_rows = pltpu.make_async_copy(orbitals, slab.at[q], local_sem.at[0])
    own_targets = pltpu.make_async_copy(targets, target_rows.at[q], local_sem.at[1])
    own_points = pltpu.make_async_copy(points, index.at[q], local_sem.at[2])
    own_weights = [
        pltpu.make_async_copy(
            potential.at[pl.ds(pl.multiple_of(where(block) * rows, rows), rows), :], weights.at[block],
            local_sem.at[3 + block])
        for block in range(groups)
    ]
    own_points.start()
    own_rows.start()
    own_targets.start()
    for copy in own_weights:
        copy.start()

    barrier = pltpu.get_barrier_semaphore()

    def greet(grid, group):
        pl.semaphore_signal(barrier, inc=1, device_id={"grid": grid, "ipts": group}, device_id_type=MESH)

    greet(g, inward)
    pl.when(q > 0)(lambda: greet(g, outward))
    greet(partner, z)
    for step in range(1, lanes):
        greet(peer(step), z)
    pl.semaphore_wait(barrier, lanes + 1 + q)

    def finish():
        for copy in sent:
            copy.wait_send()
        sent.clear()

    halves = range(SPLIT)

    def end():
        own_points.wait()
        send("index", index.at[0], index.at[0], inward)
        send("early rows", orbitals.at[:, last], slab.at[0, :, last], inward)
        send("targets", targets, target_rows.at[0], inward)
        for k in range(pieces):
            send(("end", k), orbitals.at[:, cols(k)], slab.at[0, :, cols(k)], inward)
        for half in halves:
            part = pl.ds(pl.multiple_of(where(1) * rows + half * sub, sub), sub)
            send(("lent", half), potential.at[part, :], lent.at[pl.ds(half * sub, sub), :], inward)

        views = [lambda p: values.at[0, p, last]]
        views += [lambda p, k=k: values.at[0, p, cols(k)] for k in range(pieces)]
        views += [lambda p: target_values.at[0, p, :]]
        order = [0, pieces + 1] + list(range(1, pieces + 1))
        for n, item in enumerate(order):
            receive(("value", item), views[item](place(g)))
            spread(item, views[item])
            if n > 0:
                forward(order[n - 1], views[order[n - 1]])
        forward(order[-1], views[order[-1]])
        own_rows.wait()
        own_targets.wait()
        for copy in own_weights:
            copy.wait()
        for k in range(pieces):
            receive(("out", 2, k), slab.at[2, :, cols(k)])
            receive(("out", 3, k), slab.at[3, :, cols(k)])
        for item in order:
            gathered(item, views[item])
        for half in halves:
            part = pl.ds(half * sub, sub)
            for block in (3, 2):
                receive(("out rows", block, half), slab.at[block, part, last])
                leaving[block - 2, part, :] = contribution(block, half, 0, weights.at[block]).astype(BF16)
                send(("sum", block, half), leaving.at[block - 2, part, :], arriving.at[block - 2, part, :], inward)
        for half in halves:
            kept[pl.ds(half * sub, sub), :] = contribution(0, half, 0, weights.at[0])
        for half in halves:
            part = pl.ds(half * sub, sub)
            receive(("end sum", half), arriving.at[0, part, :])
            out[part, :] = (-(kept[part, :] + arriving[0, part, :].astype(F32))).astype(out.dtype)
        finish()

    def inner():
        own_points.wait()
        send("index in", index.at[1], index.at[2], inward)
        for k in range(pieces - 1):
            send(("own", k), orbitals.at[:, cols(k)], slab.at[2, :, cols(k)], inward)
        receive("index", index.at[0])
        send("index end", index.at[0], index.at[3], inward)

        def relay(k):
            receive(("own", k), slab.at[2, :, cols(k)])
            send(("out", 2, k), slab.at[2, :, cols(k)], slab.at[2, :, cols(k)], outward)

        def cross(k):
            receive(("end", k), slab.at[0, :, cols(k)])
            send(("end in", k), slab.at[0, :, cols(k)], slab.at[3, :, cols(k)], inward)

        def mark(ref, pair, blocks):
            lane = lax.broadcasted_iota(jnp.int32, (count, LANES), 1)
            for n, group in enumerate(pair):
                wide = jnp.broadcast_to(index[group], (LANES, count)).T
                for block in range(blocks):
                    start = (g * groups + where(block)) * rows
                    for c in range(rows // LANES):
                        chosen = (wide == lane + (start + c * LANES)).astype(F32).astype(BF16)
                        ref[pl.ds(n * count, count), pl.ds(block * rows + c * LANES, LANES)] = chosen

        def pick(ref, blocks, rows_of):
            return sum(
                jnp.dot(ref[:, pl.ds(block * rows, rows)], rows_of(block), preferred_element_type=F32)
                for block in range(blocks))

        mark(hot, (1, 0), groups)
        ahead = max(pieces - 2, 0)
        for k in range(ahead):
            relay(k)
        receive("index in", index.at[2])
        receive("index end", index.at[3])
        mark(far_hot, (2, 3), 2)
        own_rows.wait()
        own_targets.wait()
        receive("early rows", slab.at[0, :, last])
        receive("targets", target_rows.at[0])
        early_out[:, pl.ds(0, early)] = pick(far_hot, 2, lambda b: slab[b, :, last]).astype(BF16)
        early_out[:, pl.ds(early, nj)] = pick(far_hot, 2, lambda b: target_rows[b]).astype(BF16)
        send("early", early_out, early_in, inward)
        early_near[:, pl.ds(0, early)] = pick(hot, 2, lambda b: slab[b, :, last]).astype(BF16)
        early_near[:, pl.ds(early, nj)] = pick(hot, 2, lambda b: target_rows[b]).astype(BF16)
        for k in range(ahead, pieces - 1):
            relay(k)
        cross(0)
        send(("own", pieces - 1), orbitals.at[:, cols(pieces - 1)], slab.at[2, :, cols(pieces - 1)], inward)

        views = [lambda p: values.at[:, p, last]]
        views += [lambda p, k=k: values.at[:, p, cols(k)] for k in range(pieces)]
        views += [lambda p: target_values.at[:, p, :]]

        receive("early", early_in)
        found = early_near[...].astype(F32) + early_in[...].astype(F32)
        for n in range(2):
            part = slice(n * count, (n + 1) * count)
            values[n, place(g), last] = found[part, :early].astype(BF16)
            target_values[n, place(g), :] = found[part, early:].astype(BF16)
        send(("value", 0), values.at[1, place(g), last], values.at[0, place(g), last], outward)
        send(("value", pieces + 1), target_values.at[1, place(g), :], target_values.at[0, place(g), :], outward)
        spread(0, views[0])
        spread(pieces + 1, views[pieces + 1])
        ready = 1

        order = [0, pieces + 1]
        for k in range(pieces):
            while ready < min(k + 3, pieces):
                cross(ready)
                ready += 1
                if ready == pieces:
                    for half in halves:
                        part = pl.ds(half * sub, sub)
                        for block in (0, 1):
                            send(("rows in", 3 - block, half), slab.at[block, part, last],
                                 slab.at[3 - block, part, last], inward)
            if k == 0:
                relay(pieces - 1)
            receive(("end in", k), slab.at[3, :, cols(k)])
            send(("out", 3, k), slab.at[3, :, cols(k)], slab.at[3, :, cols(k)], outward)
            found = pick(hot, groups, lambda b: slab[b, :, cols(k)])
            for n in range(2):
                values[n, place(g), cols(k)] = found[n * count:(n + 1) * count].astype(BF16)
            send(("value", k + 1), values.at[1, place(g), cols(k)], values.at[0, place(g), cols(k)], outward)
            spread(k + 1, views[k + 1])
            for item in order:
                forward(item, views[item])
            order = [k + 1]

        def pass_on(half):
            part = pl.ds(half * sub, sub)
            for block in (3, 2):
                receive(("rows in", block, half), slab.at[block, part, last])
                send(("out rows", block, half), slab.at[block, part, last], slab.at[block, part, last], outward)

        pass_on(0)
        forward(pieces, views[pieces])
        for half in halves[1:]:
            pass_on(half)
        for copy in own_weights:
            copy.wait()
        for item in range(pieces + 2):
            gathered(item, views[item])
        for half in halves:
            part = pl.ds(half * sub, sub)
            for block in (3, 2):
                mine = contribution(block, half, 0, weights.at[block])
                receive(("sum", block, half), arriving.at[block - 2, part, :])
                leaving[block - 2, part, :] = (mine + arriving[block - 2, part, :].astype(F32)).astype(BF16)
                send(("sum in", block, half), leaving.at[block - 2, part, :], crossing.at[3 - block, part, :], inward)
        for half in halves:
            kept_end[pl.ds(half * sub, sub), :] = contribution(0, half, 0, weights.at[0])
        for half in halves:
            part = pl.ds(half * sub, sub)
            receive(("sum in", 3, half), crossing.at[0, part, :])
            leaving[2, part, :] = (kept_end[part, :] + crossing[0, part, :].astype(F32)).astype(BF16)
            send(("end sum", half), leaving.at[2, part, :], arriving.at[0, part, :], outward)
            kept[part, :] = contribution(1, half, 0, weights.at[1])
            receive(("lent", half), lent.at[part, :])
            kept[part, :] += contribution(1, half, 1, lent)
        for half in halves:
            part = pl.ds(half * sub, sub)
            receive(("sum in", 2, half), crossing.at[1, part, :])
            out[part, :] = (-(kept[part, :] + crossing[1, part, :].astype(F32))).astype(out.dtype)
        finish()

    pl.when(q == 0)(end)
    pl.when(q == 1)(inner)


def local(orbitals, targets, points, potential):
    groups, slabs = lax.axis_size("ipts"), lax.axis_size("grid")
    assert groups == 4 and slabs % 2 == 0
    rows, norb = orbitals.shape
    nj = targets.shape[1]
    count = points.shape[1]
    early = norb // EARLY
    pieces = (norb - early) // LANES
    transfers = 12 + 6 * pieces + 20 * SPLIT
    dma = pltpu.SemaphoreType.DMA
    return pl.pallas_call(
        functools.partial(kernel, groups, slabs),
        out_shape=jax.ShapeDtypeStruct((rows, nj), BF16),
        in_specs=[pl.BlockSpec(memory_space=pl.ANY)] * 4,
        out_specs=pl.BlockSpec(memory_space=pltpu.VMEM),
        scratch_shapes=[
            pltpu.VMEM((groups, rows, norb), BF16),
            pltpu.VMEM((2, slabs * count, norb), BF16),
            pltpu.VMEM((2, slabs * count, nj), BF16),
            pltpu.VMEM((groups, rows, slabs * count), BF16),
            pltpu.VMEM((rows, slabs * count), BF16),
            pltpu.VMEM((2, rows, nj), BF16),
            pltpu.VMEM((groups, 1, count), jnp.int32),
            pltpu.VMEM((2 * count, groups * rows), BF16),
            pltpu.VMEM((2 * count, 2 * rows), BF16),
            pltpu.VMEM((2 * count, early + nj), BF16),
            pltpu.VMEM((2 * count, early + nj), BF16),
            pltpu.VMEM((2 * count, early + nj), BF16),
            pltpu.VMEM((3, rows, nj), BF16),
            pltpu.VMEM((2, rows, nj), BF16),
            pltpu.VMEM((2, rows, nj), BF16),
            pltpu.VMEM((rows, nj), F32),
            pltpu.VMEM((rows, nj), F32),
            dma((3 + groups,)),
            dma((transfers,)),
            dma((transfers,)),
            dma((pieces + 2, slabs)),
            dma((pieces + 2, slabs)),
        ],
        compiler_params=pltpu.CompilerParams(
            collective_id=0, has_side_effects=True, vmem_limit_bytes=63 * 1024 * 1024),
    )(orbitals, targets, points, potential)


def solution(mesh):
    placed = (
        P(("grid", "ipts"), None),
        P(("grid", "ipts"), None),
        P("ipts", "grid"),
        P("grid", "ipts"),
    )
    return jax.shard_map(
        local, mesh=mesh, in_specs=placed, out_specs=P(("grid", "ipts"), None), check_vma=False
    )
```

```python
import functools

import jax
import jax.numpy as jnp
from jax import lax
from jax.experimental import pallas as pl
from jax.experimental.pallas import tpu as pltpu
from jax.sharding import PartitionSpec as P

MESH = pl.DeviceIdType.MESH
LANES = 128
WIDTH = 1024
SPLIT = 2
EARLY = 4
SORTS = ("index", "slab", "targets", "lent", "near", "early", "values", "target values", "sums")
F32, BF16 = jnp.float32, jnp.bfloat16


class Names:
    def __init__(self, size):
        self.size, self.known = size, ({}, {})

    def __getitem__(self, key):
        kind, name = key
        number = self.known[kind].setdefault(name, len(self.known[kind]))
        assert number < self.size
        return number


def kernel(groups, slabs, orbitals, targets, points, potential, out,
           slab, values, target_values, weights, lent, target_rows, index, hot, far_hot,
           early_out, early_near, early_in, near_out, near_in, leaving, arriving, crossing, kept,
           local_sem, send_sem, recv_sem, plane_send, plane_recv, partner_recv):
    g = lax.axis_index("grid")
    z = lax.axis_index("ipts")
    side = z // 2
    q = z + side * (groups - 1 - 2 * z)
    inward, outward = z + 1 - 2 * side, z - 1 + 2 * side
    rows, norb = orbitals.shape
    nj = targets.shape[1]
    count = points.shape[1]
    total = slabs * count
    lanes = slabs // 2
    lane, core = g // 2, lax.rem(g, 2)
    partner = g + 1 - 2 * core
    bits = [1 << n for n in range(lanes.bit_length() - 1)]
    orders = (bits, bits[::-1])
    early = norb // EARLY
    tail = norb - early
    pieces = tail // LANES
    sub = rows // SPLIT
    quarter = sub // 2
    width = min(WIDTH, total)
    names = Names(recv_sem.shape[0])

    def where(block):
        return block + side * (groups - 1 - 2 * block)

    def cols(k):
        return pl.ds(k * LANES, LANES)

    last = pl.ds(tail, early)

    def place(slab_index):
        return pl.ds(pl.multiple_of(slab_index * count, count), count)

    def flipped(mask, of_core):
        there = lane
        for bit in bits:
            if mask & bit:
                there = there + bit - 2 * bit * lax.rem(lane // bit, 2)
        return 2 * there + of_core

    def send(kind, name, sort, src, dst, target):
        pltpu.make_async_remote_copy(
            src_ref=src, dst_ref=dst, send_sem=send_sem.at[SORTS.index(sort)], recv_sem=recv_sem.at[names[kind, name]],
            device_id={"grid": g, "ipts": target}, device_id_type=MESH).start()

    def receive(kind, name, dst):
        pltpu.make_async_copy(dst, dst, recv_sem.at[names[kind, name]]).wait()

    def left(sort, *views):
        for view in views:
            pltpu.make_async_copy(view, view, send_sem.at[SORTS.index(sort)]).wait()

    wide = pieces + 1

    def pass_to(block, item, way, target):
        recv = partner_recv.at[item // wide] if way is None else plane_recv.at[item, way - 1]
        pltpu.make_async_remote_copy(
            src_ref=block, dst_ref=block, send_sem=plane_send.at[item // wide], recv_sem=recv,
            device_id={"grid": target, "ipts": z}, device_id_type=MESH).start()

    def ways(mask, slots):
        if mask in bits:
            return [(mask, None)]
        return [(mask + slot * lanes, slot) for slot in range(slots)]

    def spread(item, view, slots):
        for bit in bits:
            pass_to(view(None, place(g)), item, bit, flipped(bit, core))
        pass_to(view(None, place(g)), item, None, partner)

    def forward(item, view, slots, single):
        masks = [m for m in range(1, lanes) if (m in bits) == single]
        for mask in sorted(masks, key=lambda m: m.bit_count()):
            for way, slot in ways(mask, slots):
                block = view(slot, place(flipped(mask, core)))
                pltpu.make_async_copy(block, block, plane_recv.at[item, way - 1]).wait()
                for n in range(slots) if slot is None else (slot,):
                    order = orders[n]
                    top = max(order.index(bit) for bit in bits if mask & bit)
                    for bit in order[top + 1:]:
                        pass_to(view(n, place(flipped(mask, core))), item, (mask | bit) + n * lanes, flipped(bit, core))
                pass_to(block, item, None, partner)

    def all_of(blocks, pick):
        several = pl.ds(0, blocks * count)
        return (values.at[pick, several, :], target_values.at[pick, several, :])

    def gathered(pick):
        for n, view in enumerate(all_of(lanes, pick)):
            pltpu.make_async_copy(view, view, partner_recv.at[n]).wait()

    def passed(pick):
        for n, view in enumerate(all_of(slabs - 1, pick)):
            pltpu.make_async_copy(view, view, plane_send.at[n]).wait()

    def contribution(block, half, slot, kernel_rows):
        part = pl.ds(half * sub, sub)
        acc = None
        for start in range(0, total, width):
            some = pl.ds(start, width)
            products = lax.dot_general(
                slab[block, part, :], values[slot, some, :], (((1,), (1,)), ((), ())),
                preferred_element_type=F32)
            weighted = (kernel_rows[part, some].astype(F32) * products).astype(BF16)
            term = jnp.dot(weighted, target_values[slot, some, :], preferred_element_type=F32)
            acc = term if acc is None else acc + term
        return acc

    own_rows = pltpu.make_async_copy(orbitals, slab.at[q], local_sem.at[0])
    own_targets = pltpu.make_async_copy(targets, target_rows.at[q], local_sem.at[1])
    own_points = pltpu.make_async_copy(points, index.at[q], local_sem.at[2])
    own_weights = [
        pltpu.make_async_copy(
            potential.at[pl.ds(pl.multiple_of(where(block) * rows, rows), rows), :], weights.at[block],
            local_sem.at[3 + block])
        for block in range(groups)
    ]
    own_points.start()
    own_rows.start()
    own_targets.start()
    for copy in own_weights:
        copy.start()

    barrier = pltpu.get_barrier_semaphore()

    def greet(grid, group):
        pl.semaphore_signal(barrier, inc=1, device_id={"grid": grid, "ipts": group}, device_id_type=MESH)

    greet(g, inward)
    pl.when(q > 0)(lambda: greet(g, outward))
    greet(partner, z)
    for bit in bits:
        greet(flipped(bit, core), z)
    pl.semaphore_wait(barrier, len(bits) + 2 + q)

    halves = range(SPLIT)

    quarters = [(2 * half, 2 * half + 1) for half in halves]

    def few(n):
        return pl.ds(n * quarter, quarter)

    def mark(ref, marked, blocks):
        spot = lax.broadcasted_iota(jnp.int32, (count, LANES), 1)
        for n, group in enumerate(marked):
            wanted = jnp.broadcast_to(index[group], (LANES, count)).T
            for m, block in enumerate(blocks):
                start = (g * groups + where(block)) * rows
                for c in range(rows // LANES):
                    chosen = (wanted == spot + (start + c * LANES)).astype(F32).astype(BF16)
                    ref[pl.ds(n * count, count), pl.ds(m * rows + c * LANES, LANES)] = chosen

    def pick(marks, blocks, rows_of):
        return sum(
            jnp.dot(marks[:, pl.ds(m * rows, rows)], rows_of(block), preferred_element_type=F32)
            for m, block in enumerate(blocks))

    def end():
        own_points.wait()
        send(1, "index", "index", index.at[0], index.at[0], inward)
        send(1, "early rows", "slab", orbitals.at[:, last], slab.at[0, :, last], inward)
        send(1, "targets", "targets", targets, target_rows.at[0], inward)
        for k in range(pieces):
            send(1, ("end", k), "slab", orbitals.at[:, cols(k)], slab.at[0, :, cols(k)], inward)
        for half in halves:
            part = pl.ds(pl.multiple_of(where(1) * rows + half * sub, sub), sub)
            send(1, ("lent", half), "lent", potential.at[part, :], lent.at[pl.ds(half * sub, sub), :], inward)

        views = [lambda n, p: values.at[0, p, last]]
        views += [lambda n, p, k=k: values.at[0, p, cols(k)] for k in range(pieces)]
        views += [lambda n, p: target_values.at[0, p, :]]
        marks = hot.at[pl.ds(0, count), :]
        mark(marks, (0,), (0, 2, 3))
        own_rows.wait()
        receive(0, "near", near_in)
        for item in (0, wide):
            receive(0, ("value", item), views[item](0, place(g)))
            spread(item, views[item], 1)
        before, older = [0, wide], []
        for k in range(pieces):
            for block in (2, 3):
                receive(0, ("out", block, k), slab.at[block, :, cols(k)])
            found = pick(marks, (0, 2, 3), lambda block: slab[block, :, cols(k)])
            values[0, place(g), cols(k)] = (found + near_in[:, cols(k)].astype(F32)).astype(BF16)
            spread(k + 1, views[k + 1], 1)
            for item in before:
                forward(item, views[item], 1, True)
            for item in older:
                forward(item, views[item], 1, False)
            before, older = [k + 1], before
        for item in before:
            forward(item, views[item], 1, True)
        for item in older + before:
            forward(item, views[item], 1, False)
        own_targets.wait()
        for copy in own_weights:
            copy.wait()
        gathered(0)
        for block in (3, 2):
            for half in halves:
                part = pl.ds(half * sub, sub)
                receive(0, ("out rows", block, half), slab.at[block, part, last])
                leaving[block - 2, part, :] = contribution(block, half, 0, weights.at[block]).astype(BF16)
                for n in quarters[half]:
                    send(1, ("sum", block, n), "sums", leaving.at[block - 2, few(n), :],
                         arriving.at[block - 2, few(n), :], inward)
        for half in halves:
            kept[0, pl.ds(half * sub, sub), :] = contribution(0, half, 0, weights.at[0])
        for n in range(2 * SPLIT):
            receive(0, ("end sum", n), arriving.at[0, few(n), :])
            out[few(n), :] = (-(kept[0, few(n), :] + arriving[0, few(n), :].astype(F32))).astype(out.dtype)
        left("index", index.at[0])
        left("slab", slab.at[0])
        left("targets", target_rows.at[0])
        left("lent", lent)
        left("sums", leaving.at[pl.ds(0, 2)])
        passed(0)

    def inner():
        both = pl.ds(0, 2)
        own_points.wait()
        send(1, "index in", "index", index.at[1], index.at[2], inward)

        def own(k):
            send(1, ("own", k), "slab", orbitals.at[:, cols(k)], slab.at[2, :, cols(k)], inward)

        own(0)
        receive(1, "index", index.at[0])
        send(1, "index end", "index", index.at[0], index.at[3], inward)
        for k in range(1, pieces):
            own(k)

        def relay(block, k):
            send(0, ("out", block, k), "slab", slab.at[block, :, cols(k)], slab.at[block, :, cols(k)], outward)

        def relay_own(k):
            receive(1, ("own", k), slab.at[2, :, cols(k)])
            relay(2, k)

        def cross(k):
            receive(1, ("end", k), slab.at[0, :, cols(k)])
            send(1, ("end in", k), "slab", slab.at[0, :, cols(k)], slab.at[3, :, cols(k)], inward)

        mark(hot, (1, 0), range(groups))
        own_rows.wait()
        near_out[...] = jnp.dot(
            hot[pl.ds(count, count), pl.ds(rows, rows)], slab[1, :, pl.ds(0, tail)],
            preferred_element_type=F32).astype(BF16)
        send(0, "near", "near", near_out, near_in, outward)
        ahead = max(pieces - 2, 0)
        for k in range(ahead):
            relay_own(k)
        receive(1, "index in", index.at[2])
        receive(1, "index end", index.at[3])
        mark(far_hot, (2, 3), (0, 1))
        own_targets.wait()
        receive(1, "early rows", slab.at[0, :, last])
        receive(1, "targets", target_rows.at[0])
        early_out[:, pl.ds(0, early)] = pick(far_hot, (0, 1), lambda b: slab[b, :, last]).astype(BF16)
        early_out[:, pl.ds(early, nj)] = pick(far_hot, (0, 1), lambda b: target_rows[b]).astype(BF16)
        send(1, "early", "early", early_out, early_in, inward)
        early_near[:, pl.ds(0, early)] = pick(hot, (0, 1), lambda b: slab[b, :, last]).astype(BF16)
        early_near[:, pl.ds(early, nj)] = pick(hot, (0, 1), lambda b: target_rows[b]).astype(BF16)
        for k in range(ahead, pieces):
            relay_own(k)
        ready = min(pieces, 3)
        for k in range(ready):
            cross(k)

        views = [lambda n, p: values.at[both if n is None else n, p, last]]
        views += [lambda n, p, k=k: values.at[both if n is None else n, p, cols(k)] for k in range(pieces)]
        views += [lambda n, p: target_values.at[both if n is None else n, p, :]]

        receive(1, "early", early_in)
        found = early_near[...].astype(F32) + early_in[...].astype(F32)
        for n in range(2):
            part = slice(n * count, (n + 1) * count)
            values[n, place(g), last] = found[part, :early].astype(BF16)
            target_values[n, place(g), :] = found[part, early:].astype(BF16)
        send(0, ("value", 0), "values", values.at[1, place(g), last], values.at[0, place(g), last], outward)
        send(0, ("value", wide), "target values", target_values.at[1, place(g), :],
             target_values.at[0, place(g), :], outward)
        spread(0, views[0], 2)
        spread(wide, views[wide], 2)

        def rows_in():
            for block in (0, 1):
                for half in halves:
                    part = pl.ds(half * sub, sub)
                    send(1, ("rows in", 3 - block, half), "slab", slab.at[block, part, last],
                         slab.at[3 - block, part, last], inward)

        before, older = [0, wide], []
        for k in range(pieces):
            while ready < min(pieces, 5 + k):
                cross(ready)
                ready += 1
                if ready == pieces:
                    rows_in()
            receive(1, ("end in", k), slab.at[3, :, cols(k)])
            relay(3, k)
            found = pick(hot, range(groups), lambda b: slab[b, :, cols(k)])
            for n in range(2):
                values[n, place(g), cols(k)] = found[n * count:(n + 1) * count].astype(BF16)
            spread(k + 1, views[k + 1], 2)
            for item in before:
                forward(item, views[item], 2, True)
            for item in older:
                forward(item, views[item], 2, False)
            before, older = [k + 1], before

        def pass_on(block):
            for half in halves:
                part = pl.ds(half * sub, sub)
                receive(1, ("rows in", block, half), slab.at[block, part, last])
                send(0, ("out rows", block, half), "slab", slab.at[block, part, last],
                     slab.at[block, part, last], outward)

        pass_on(3)
        for item in before:
            forward(item, views[item], 2, True)
        for item in older + before:
            forward(item, views[item], 2, False)
        pass_on(2)
        for copy in own_weights:
            copy.wait()
        gathered(both)

        def keep(block, half, slot, kernel_rows):
            part = pl.ds(half * sub, sub)
            kept[block, part, :] = contribution(block, half, slot, kernel_rows)

        def sums(block, half):
            for n in quarters[half]:
                receive(1, ("sum", block, n), arriving.at[block - 2, few(n), :])
                leaving[block - 2, few(n), :] = (
                    kept[block, few(n), :] + arriving[block - 2, few(n), :].astype(F32)).astype(BF16)
                send(1, ("sum in", block, n), "sums", leaving.at[block - 2, few(n), :],
                     crossing.at[3 - block, few(n), :], inward)

        def end_sums(half):
            for n in quarters[half]:
                receive(1, ("sum in", 3, n), crossing.at[0, few(n), :])
                leaving[2, few(n), :] = (kept[0, few(n), :] + crossing[0, few(n), :].astype(F32)).astype(BF16)
                send(0, ("end sum", n), "sums", leaving.at[2, few(n), :], arriving.at[0, few(n), :], outward)

        def near(half):
            part = pl.ds(half * sub, sub)
            keep(1, half, 0, weights.at[1])
            receive(1, ("lent", half), lent.at[part, :])
            kept[1, part, :] += contribution(1, half, 1, lent)

        for block in (3, 2):
            for half in halves:
                keep(block, half, 0, weights.at[block])
                if half > 0:
                    sums(block, half - 1)
            if block == 2:
                for half in halves:
                    keep(0, half, 0, weights.at[0])
            for half in halves:
                if block == 2:
                    end_sums(half)
            sums(block, SPLIT - 1)
        for half in halves:
            near(half)
        for n in range(2 * SPLIT):
            receive(1, ("sum in", 2, n), crossing.at[1, few(n), :])
            out[few(n), :] = (-(kept[1, few(n), :] + crossing[1, few(n), :].astype(F32))).astype(out.dtype)
        left("index", index.at[both])
        left("slab", slab)
        left("near", near_out)
        left("early", early_out)
        left("values", values.at[0, pl.ds(0, count), last])
        left("target values", target_values.at[0, pl.ds(0, count), :])
        left("sums", leaving)
        passed(both)

    pl.when(q == 0)(end)
    pl.when(q == 1)(inner)


def local(orbitals, targets, points, potential):
    groups, slabs = lax.axis_size("ipts"), lax.axis_size("grid")
    assert groups == 4 and slabs.bit_count() == 1
    rows, norb = orbitals.shape
    nj = targets.shape[1]
    count = points.shape[1]
    early = norb // EARLY
    pieces = (norb - early) // LANES
    transfers = 6 + 3 * pieces + 11 * SPLIT
    lanes = slabs // 2
    dma = pltpu.SemaphoreType.DMA
    return pl.pallas_call(
        functools.partial(kernel, groups, slabs),
        out_shape=jax.ShapeDtypeStruct((rows, nj), BF16),
        in_specs=[pl.BlockSpec(memory_space=pl.ANY)] * 4,
        out_specs=pl.BlockSpec(memory_space=pltpu.VMEM),
        scratch_shapes=[
            pltpu.VMEM((groups, rows, norb), BF16),
            pltpu.VMEM((2, slabs * count, norb), BF16),
            pltpu.VMEM((2, slabs * count, nj), BF16),
            pltpu.VMEM((groups, rows, slabs * count), BF16),
            pltpu.VMEM((rows, slabs * count), BF16),
            pltpu.VMEM((2, rows, nj), BF16),
            pltpu.VMEM((groups, 1, count), jnp.int32),
            pltpu.VMEM((2 * count, groups * rows), BF16),
            pltpu.VMEM((2 * count, 2 * rows), BF16),
            pltpu.VMEM((2 * count, early + nj), BF16),
            pltpu.VMEM((2 * count, early + nj), BF16),
            pltpu.VMEM((2 * count, early + nj), BF16),
            pltpu.VMEM((count, norb - early), BF16),
            pltpu.VMEM((count, norb - early), BF16),
            pltpu.VMEM((3, rows, nj), BF16),
            pltpu.VMEM((2, rows, nj), BF16),
            pltpu.VMEM((2, rows, nj), BF16),
            pltpu.VMEM((groups, rows, nj), F32),
            dma((3 + groups,)),
            dma((len(SORTS),)),
            dma((transfers,)),
            dma((2,)),
            dma((pieces + 2, 2 * lanes - 1)),
            dma((2,)),
        ],
        compiler_params=pltpu.CompilerParams(
            collective_id=0, has_side_effects=True, vmem_limit_bytes=63 * 1024 * 1024),
    )(orbitals, targets, points, potential)


def solution(mesh):
    placed = (
        P(("grid", "ipts"), None),
        P(("grid", "ipts"), None),
        P("ipts", "grid"),
        P("grid", "ipts"),
    )
    return jax.shard_map(
        local, mesh=mesh, in_specs=placed, out_specs=P(("grid", "ipts"), None), check_vma=False
    )
```

```python
import functools
import math

import jax
import jax.numpy as jnp
from jax import lax
from jax.experimental import pallas as pl
from jax.experimental.pallas import tpu as pltpu
from jax.sharding import PartitionSpec as P

MESH = pl.DeviceIdType.MESH
LANES = 128
WIDTH = 1024
SPLIT = 2
EARLY = (3, 8)
DIRECT = 2
LOANS = 8
ROOM, MOST = 8 << 20, 63 << 20
SORTS = ("index", "slab", "targets", "lent", "near", "early", "values", "target values", "sums")
F32, BF16 = jnp.float32, jnp.bfloat16


class Names:
    def __init__(self, size):
        self.size, self.known = size, ({}, {})

    def __getitem__(self, key):
        kind, name = key
        number = self.known[kind].setdefault(name, len(self.known[kind]))
        assert number < self.size
        return number


def kernel(groups, slabs, orbitals, targets, points, potential, out,
           slab, values, target_values, weights, lent, target_rows, index, hot, far_hot,
           early_out, early_near, early_in, near_out, near_in, leaving, arriving, crossing, kept,
           local_sem, send_sem, recv_sem, plane_send, plane_recv, partner_recv):
    g = lax.axis_index("grid")
    z = lax.axis_index("ipts")
    side = z // 2
    q = z + side * (groups - 1 - 2 * z)
    inward, outward = z + 1 - 2 * side, z - 1 + 2 * side
    rows, norb = orbitals.shape
    nj = targets.shape[1]
    count = points.shape[1]
    total = slabs * count
    lanes = slabs // 2
    lane, core = g // 2, lax.rem(g, 2)
    partner = g + 1 - 2 * core
    bits = [1 << n for n in range(lanes.bit_length() - 1)]
    orders = (bits, bits[::-1])
    early = norb * EARLY[0] // EARLY[1]
    tail = norb - early
    pieces = tail // LANES
    sub = rows // SPLIT
    quarter = sub // 2
    loan = rows // LOANS
    width = min(WIDTH, total)
    names = Names(recv_sem.shape[0])

    def where(block):
        return block + side * (groups - 1 - 2 * block)

    def cols(k):
        return pl.ds(k * LANES, LANES)

    last = pl.ds(tail, early)

    def place(slab_index):
        return pl.ds(pl.multiple_of(slab_index * count, count), count)

    def flipped(mask, of_core):
        there = lane
        for bit in bits:
            if mask & bit:
                there = there + bit - 2 * bit * lax.rem(lane // bit, 2)
        return 2 * there + of_core

    def send(kind, name, sort, src, dst, target):
        pltpu.make_async_remote_copy(
            src_ref=src, dst_ref=dst, send_sem=send_sem.at[SORTS.index(sort)], recv_sem=recv_sem.at[names[kind, name]],
            device_id={"grid": g, "ipts": target}, device_id_type=MESH).start()

    def receive(kind, name, dst):
        pltpu.make_async_copy(dst, dst, recv_sem.at[names[kind, name]]).wait()

    def left(sort, *views):
        for view in views:
            pltpu.make_async_copy(view, view, send_sem.at[SORTS.index(sort)]).wait()

    wide = pieces + 1
    direct = max(pieces - DIRECT, 1)

    def pass_to(block, item, way, target):
        recv = partner_recv.at[item // wide] if way is None else plane_recv.at[item, way]
        pltpu.make_async_remote_copy(
            src_ref=block, dst_ref=block, send_sem=plane_send.at[item // wide], recv_sem=recv,
            device_id={"grid": target, "ipts": z}, device_id_type=MESH).start()

    routed = [mask for mask in range(1, lanes) if mask not in bits]

    def way_of(mask, slot):
        if mask in bits:
            return bits.index(mask)
        return len(bits) + slot * len(routed) + routed.index(mask)

    def ways(mask, slots):
        if mask in bits:
            return [(way_of(mask, None), None)]
        return [(way_of(mask, slot), slot) for slot in range(slots)]

    def spread(item, view, slots):
        for bit in bits:
            pass_to(view(None, place(g)), item, way_of(bit, None), flipped(bit, core))
        pass_to(view(None, place(g)), item, None, partner)

    def spread_straight(item, view):
        for mask in range(1, lanes):
            pass_to(view(0, place(g)), item, way_of(mask, 0), flipped(mask, core))
        pass_to(view(0, place(g)), item, None, partner)

    def hand_over(item, view):
        for mask in range(1, lanes):
            block = view(0, place(flipped(mask, core)))
            pltpu.make_async_copy(block, block, plane_recv.at[item, way_of(mask, 0)]).wait()
            pass_to(block, item, None, partner)

    def forward(item, view, slots, single):
        masks = [m for m in range(1, lanes) if (m in bits) == single]
        for mask in sorted(masks, key=lambda m: m.bit_count()):
            for way, slot in ways(mask, slots):
                block = view(slot, place(flipped(mask, core)))
                pltpu.make_async_copy(block, block, plane_recv.at[item, way]).wait()
                for n in range(slots) if slot is None else (slot,):
                    order = orders[n]
                    top = max(order.index(bit) for bit in bits if mask & bit)
                    for bit in order[top + 1:]:
                        pass_to(view(n, place(flipped(mask, core))), item, way_of(mask | bit, n), flipped(bit, core))
                pass_to(block, item, None, partner)

    def all_of(blocks, pick):
        several = pl.ds(0, blocks * count)
        return (values.at[pick, several, :], target_values.at[pick, several, :])

    def gathered(pick):
        for n, view in enumerate(all_of(lanes, pick)):
            pltpu.make_async_copy(view, view, partner_recv.at[n]).wait()

    def passed(pick):
        for n, view in enumerate(all_of(slabs - 1, pick)):
            pltpu.make_async_copy(view, view, plane_send.at[n]).wait()

    def contribution(block, half, slot, kernel_rows):
        part = pl.ds(half * sub, sub)
        acc = None
        for start in range(0, total, width):
            some = pl.ds(start, width)
            products = lax.dot_general(
                slab[block, part, :], values[slot, some, :], (((1,), (1,)), ((), ())),
                preferred_element_type=F32)
            weighted = (kernel_rows[part, some].astype(F32) * products).astype(BF16)
            term = jnp.dot(weighted, target_values[slot, some, :], preferred_element_type=F32)
            acc = term if acc is None else acc + term
        return acc

    own_rows = pltpu.make_async_copy(orbitals, slab.at[q], local_sem.at[0])
    own_targets = pltpu.make_async_copy(targets, target_rows.at[q], local_sem.at[1])
    own_points = pltpu.make_async_copy(points, index.at[q], local_sem.at[2])
    own_weights = [
        pltpu.make_async_copy(
            potential.at[pl.ds(pl.multiple_of(where(block) * rows, rows), rows), :], weights.at[block],
            local_sem.at[3 + block])
        for block in range(groups)
    ]
    own_points.start()
    own_rows.start()
    own_targets.start()
    for copy in own_weights:
        copy.start()

    barrier = pltpu.get_barrier_semaphore()

    def greet(grid, group):
        pl.semaphore_signal(barrier, inc=1, device_id={"grid": grid, "ipts": group}, device_id_type=MESH)

    greet(g, inward)
    pl.when(q > 0)(lambda: greet(g, outward))
    greet(partner, z)
    for mask in range(1, lanes):
        if mask in bits:
            greet(flipped(mask, core), z)
        else:
            pl.when(q == 0)(lambda mask=mask: greet(flipped(mask, core), z))
    pl.semaphore_wait(barrier, jnp.where(q == 0, lanes + 1, len(bits) + 3))

    halves = range(SPLIT)

    quarters = [(2 * half, 2 * half + 1) for half in halves]

    def few(n):
        return pl.ds(n * quarter, quarter)

    def mark(ref, marked, blocks):
        spot = lax.broadcasted_iota(jnp.int32, (count, LANES), 1)
        for n, group in enumerate(marked):
            wanted = jnp.broadcast_to(index[group], (LANES, count)).T
            for m, block in enumerate(blocks):
                start = (g * groups + where(block)) * rows
                for c in range(rows // LANES):
                    chosen = (wanted == spot + (start + c * LANES)).astype(F32).astype(BF16)
                    ref[pl.ds(n * count, count), pl.ds(m * rows + c * LANES, LANES)] = chosen

    def pick(marks, blocks, rows_of):
        return sum(
            jnp.dot(marks[:, pl.ds(m * rows, rows)], rows_of(block), preferred_element_type=F32)
            for m, block in enumerate(blocks))

    def end():
        own_points.wait()
        send(1, "index", "index", index.at[0], index.at[0], inward)
        send(1, "early rows", "slab", orbitals.at[:, last], slab.at[0, :, last], inward)
        send(1, "targets", "targets", targets, target_rows.at[0], inward)
        for k in range(pieces):
            send(1, ("end", k), "slab", orbitals.at[:, cols(k)], slab.at[0, :, cols(k)], inward)

        def lend(n):
            part = pl.ds(pl.multiple_of(where(1) * rows + n * loan, loan), loan)
            send(1, ("lent", n), "lent", potential.at[part, :], lent.at[pl.ds(n * loan, loan), :], inward)

        for n in range(LOANS - 2):
            lend(n)
        views = [lambda n, p: values.at[0, p, last]]
        views += [lambda n, p, k=k: values.at[0, p, cols(k)] for k in range(pieces)]
        views += [lambda n, p: target_values.at[0, p, :]]
        marks = hot.at[pl.ds(0, count), :]
        mark(marks, (0,), (0, 2, 3))
        own_rows.wait()
        receive(0, "near", near_in)
        for item in (0, wide):
            receive(0, ("value", item), views[item](0, place(g)))
            spread_straight(item, views[item])
        waiting = [0, wide]
        for k in range(pieces):
            if k < direct:
                for block in (2, 3):
                    receive(0, ("out", block, k), slab.at[block, :, cols(k)])
                found = pick(marks, (0, 2, 3), lambda block: slab[block, :, cols(k)])
                values[0, place(g), cols(k)] = (found + near_in[:, cols(k)].astype(F32)).astype(BF16)
            else:
                receive(0, ("value", k + 1), views[k + 1](0, place(g)))
            spread_straight(k + 1, views[k + 1])
            while len(waiting) > 1:
                item = waiting.pop(0)
                hand_over(item, views[item])
            waiting.append(k + 1)
        for item in waiting:
            hand_over(item, views[item])
        own_targets.wait()
        for copy in own_weights:
            copy.wait()
        gathered(0)
        for k in range(direct, pieces):
            for block in (2, 3):
                receive(0, ("out", block, k), slab.at[block, :, cols(k)])
        for block in (3, 2):
            for half in halves:
                part = pl.ds(half * sub, sub)
                for n in quarters[half]:
                    receive(0, ("out rows", block, n), slab.at[block, few(n), last])
                leaving[block - 2, part, :] = contribution(block, half, 0, weights.at[block]).astype(BF16)
                for n in quarters[half]:
                    send(1, ("sum", block, n), "sums", leaving.at[block - 2, few(n), :],
                         arriving.at[block - 2, few(n), :], inward)
                if (block, half) == (3, 0):
                    lend(LOANS - 2)
        lend(LOANS - 1)
        for half in halves:
            kept[0, pl.ds(half * sub, sub), :] = contribution(0, half, 0, weights.at[0])
        for n in range(2 * SPLIT):
            receive(0, ("end sum", n), arriving.at[0, few(n), :])
            out[few(n), :] = (-(kept[0, few(n), :] + arriving[0, few(n), :].astype(F32))).astype(out.dtype)
        left("index", index.at[0])
        left("slab", slab.at[0])
        left("targets", target_rows.at[0])
        left("lent", lent)
        left("sums", leaving.at[pl.ds(0, 2)])
        passed(0)

    def inner():
        both = pl.ds(0, 2)
        own_points.wait()
        send(1, "index in", "index", index.at[1], index.at[2], inward)

        def own(k):
            send(1, ("own", k), "slab", orbitals.at[:, cols(k)], slab.at[2, :, cols(k)], inward)

        first = min(pieces, 3)
        for k in range(first):
            own(k)
        receive(1, "index", index.at[0])
        send(1, "index end", "index", index.at[0], index.at[3], inward)
        for k in range(first, pieces):
            own(k)

        def relay(block, k):
            send(0, ("out", block, k), "slab", slab.at[block, :, cols(k)], slab.at[block, :, cols(k)], outward)

        def relay_own(k):
            receive(1, ("own", k), slab.at[2, :, cols(k)])
            relay(2, k)

        def cross(k):
            receive(1, ("end", k), slab.at[0, :, cols(k)])
            send(1, ("end in", k), "slab", slab.at[0, :, cols(k)], slab.at[3, :, cols(k)], inward)

        mark(hot, (1, 0), range(groups))
        own_rows.wait()
        near_out[...] = jnp.dot(
            hot[pl.ds(count, count), pl.ds(rows, rows)], slab[1, :, pl.ds(0, direct * LANES)],
            preferred_element_type=F32).astype(BF16)
        send(0, "near", "near", near_out, near_in, outward)
        ahead = max(pieces - 2, 0)
        for k in range(ahead):
            relay_own(k)
        receive(1, "index in", index.at[2])
        receive(1, "index end", index.at[3])
        mark(far_hot, (2, 3), (0, 1))
        own_targets.wait()
        receive(1, "early rows", slab.at[0, :, last])
        orbital_part, target_part = pl.ds(0, early), pl.ds(early, nj)
        early_out[:, orbital_part] = pick(far_hot, (0, 1), lambda b: slab[b, :, last]).astype(BF16)
        send(1, "early", "early", early_out.at[:, orbital_part], early_in.at[:, orbital_part], inward)
        early_near[:, orbital_part] = pick(hot, (0, 1), lambda b: slab[b, :, last]).astype(BF16)
        for k in range(ahead, pieces):
            relay_own(k)
        receive(1, "targets", target_rows.at[0])
        early_out[:, target_part] = pick(far_hot, (0, 1), lambda b: target_rows[b]).astype(BF16)
        send(1, "early targets", "early", early_out.at[:, target_part], early_in.at[:, target_part], inward)
        early_near[:, target_part] = pick(hot, (0, 1), lambda b: target_rows[b]).astype(BF16)
        ready = 1
        cross(0)

        views = [lambda n, p: values.at[both if n is None else n, p, last]]
        views += [lambda n, p, k=k: values.at[both if n is None else n, p, cols(k)] for k in range(pieces)]
        views += [lambda n, p: target_values.at[both if n is None else n, p, :]]

        def found_early(part):
            return early_near[:, part].astype(F32) + early_in[:, part].astype(F32)

        receive(1, "early", early_in.at[:, orbital_part])
        found = found_early(orbital_part)
        for n in range(2):
            values[n, place(g), last] = found[n * count:(n + 1) * count].astype(BF16)
        send(0, ("value", 0), "values", values.at[1, place(g), last], values.at[0, place(g), last], outward)
        spread(0, views[0], 2)
        if pieces > 1:
            ready = 2
            cross(1)
        receive(1, "early targets", early_in.at[:, target_part])
        found = found_early(target_part)
        for n in range(2):
            target_values[n, place(g), :] = found[n * count:(n + 1) * count].astype(BF16)
        send(0, ("value", wide), "target values", target_values.at[1, place(g), :],
             target_values.at[0, place(g), :], outward)
        spread(wide, views[wide], 2)

        def rows_in():
            for block in (0, 1):
                for n in range(2 * SPLIT):
                    send(1, ("rows in", 3 - block, n), "slab", slab.at[block, few(n), last],
                         slab.at[3 - block, few(n), last], inward)

        batches = [[0, wide]] + [[k + 1] for k in range(pieces)]

        def onward(n, single):
            for item in batches[n]:
                forward(item, views[item], 2, single)

        for k in range(pieces):
            while ready < min(pieces, 3 + k):
                cross(ready)
                ready += 1
                if ready == pieces:
                    rows_in()
            receive(1, ("end in", k), slab.at[3, :, cols(k)])
            if k < direct:
                relay(3, k)
            found = pick(hot, range(groups), lambda b: slab[b, :, cols(k)])
            for n in range(2):
                values[n, place(g), cols(k)] = found[n * count:(n + 1) * count].astype(BF16)
            if k >= direct:
                send(0, ("value", k + 1), "values", values.at[1, place(g), cols(k)],
                     values.at[0, place(g), cols(k)], outward)
                relay(3, k)
            spread(k + 1, views[k + 1], 2)
            if k > 0:
                onward(k - 1, True)
            if k > 1:
                onward(k - 2, False)

        def pass_on(block, n):
            receive(1, ("rows in", block, n), slab.at[block, few(n), last])
            send(0, ("out rows", block, n), "slab", slab.at[block, few(n), last],
                 slab.at[block, few(n), last], outward)

        def keep(block, half, slot, kernel_rows):
            part = pl.ds(half * sub, sub)
            kept[block, part, :] = contribution(block, half, slot, kernel_rows)

        def sums(block, half):
            for n in quarters[half]:
                receive(1, ("sum", block, n), arriving.at[block - 2, few(n), :])
                leaving[block - 2, few(n), :] = (
                    kept[block, few(n), :] + arriving[block - 2, few(n), :].astype(F32)).astype(BF16)
                send(1, ("sum in", block, n), "sums", leaving.at[block - 2, few(n), :],
                     crossing.at[3 - block, few(n), :], inward)

        def end_sums(half):
            for n in quarters[half]:
                receive(1, ("sum in", 3, n), crossing.at[0, few(n), :])
                leaving[2, few(n), :] = (kept[0, few(n), :] + crossing[0, few(n), :].astype(F32)).astype(BF16)
                send(0, ("end sum", n), "sums", leaving.at[2, few(n), :], arriving.at[0, few(n), :], outward)

        def near(half):
            part = pl.ds(half * sub, sub)
            keep(1, half, 0, weights.at[1])
            for n in range(half * LOANS // SPLIT, (half + 1) * LOANS // SPLIT):
                receive(1, ("lent", n), lent.at[pl.ds(n * loan, loan), :])
            kept[1, part, :] += contribution(1, half, 1, lent)

        onward(pieces - 1, True)
        onward(pieces - 2, False)
        pass_on(3, 0)
        pass_on(3, 1)
        onward(pieces, True)
        onward(pieces - 1, False)
        pass_on(3, 2)
        onward(pieces, False)
        for copy in own_weights:
            copy.wait()
        gathered(both)
        keep(3, 0, 0, weights.at[3])
        pass_on(3, 3)
        keep(3, 1, 0, weights.at[3])
        pass_on(2, 0)
        keep(0, 0, 0, weights.at[0])
        pass_on(2, 1)
        keep(2, 0, 0, weights.at[2])
        pass_on(2, 2)
        sums(3, 0)
        pass_on(2, 3)
        keep(2, 1, 0, weights.at[2])
        keep(0, 1, 0, weights.at[0])
        sums(3, 1)
        end_sums(0)
        sums(2, 0)
        end_sums(1)
        near(0)
        sums(2, 1)
        near(1)
        for n in range(2 * SPLIT):
            receive(1, ("sum in", 2, n), crossing.at[1, few(n), :])
            out[few(n), :] = (-(kept[1, few(n), :] + crossing[1, few(n), :].astype(F32))).astype(out.dtype)
        left("index", index.at[both])
        left("slab", slab)
        left("near", near_out)
        left("early", early_out)
        left("values", values.at[0, pl.ds(0, count), pl.ds(direct * LANES, norb - direct * LANES)])
        left("target values", target_values.at[0, pl.ds(0, count), :])
        left("sums", leaving)
        passed(both)

    pl.when(q == 0)(end)
    pl.when(q == 1)(inner)


def local(orbitals, targets, points, potential):
    groups, slabs = lax.axis_size("ipts"), lax.axis_size("grid")
    assert groups == 4 and slabs.bit_count() == 1
    rows, norb = orbitals.shape
    nj = targets.shape[1]
    count = points.shape[1]
    early = norb * EARLY[0] // EARLY[1]
    pieces = (norb - early) // LANES
    transfers = 7 + 3 * pieces + 12 * SPLIT + LOANS
    lanes = slabs // 2
    doublings = lanes.bit_length() - 1
    dma = pltpu.SemaphoreType.DMA
    buffers = [
        pltpu.VMEM((groups, rows, norb), BF16),
        pltpu.VMEM((2, slabs * count, norb), BF16),
        pltpu.VMEM((2, slabs * count, nj), BF16),
        pltpu.VMEM((groups, rows, slabs * count), BF16),
        pltpu.VMEM((rows, slabs * count), BF16),
        pltpu.VMEM((2, rows, nj), BF16),
        pltpu.VMEM((groups, 1, count), jnp.int32),
        pltpu.VMEM((2 * count, groups * rows), BF16),
        pltpu.VMEM((2 * count, 2 * rows), BF16),
        pltpu.VMEM((2 * count, early + nj), BF16),
        pltpu.VMEM((2 * count, early + nj), BF16),
        pltpu.VMEM((2 * count, early + nj), BF16),
        pltpu.VMEM((count, max(pieces - DIRECT, 1) * LANES), BF16),
        pltpu.VMEM((count, max(pieces - DIRECT, 1) * LANES), BF16),
        pltpu.VMEM((3, rows, nj), BF16),
        pltpu.VMEM((2, rows, nj), BF16),
        pltpu.VMEM((2, rows, nj), BF16),
        pltpu.VMEM((groups, rows, nj), F32),
    ]
    size = sum(math.prod(b.shape) * jnp.dtype(b.dtype).itemsize for b in buffers)
    limit = min(size + ROOM, MOST)
    held = [pltpu.with_memory_space_constraint(x, pltpu.HBM) for x in (orbitals, targets, points, potential)]
    return pl.pallas_call(
        functools.partial(kernel, groups, slabs),
        out_shape=jax.ShapeDtypeStruct((rows, nj), BF16),
        in_specs=[pl.BlockSpec(memory_space=pl.ANY)] * 4,
        out_specs=pl.BlockSpec(memory_space=pltpu.VMEM),
        scratch_shapes=buffers + [
            dma((3 + groups,)),
            dma((len(SORTS),)),
            dma((transfers,)),
            dma((2,)),
            dma((pieces + 2, doublings + 2 * (lanes - 1 - doublings))),
            dma((2,)),
        ],
        compiler_params=pltpu.CompilerParams(
            collective_id=0, has_side_effects=True, vmem_limit_bytes=limit),
    )(*held)


def solution(mesh):
    placed = (
        P(("grid", "ipts"), None),
        P(("grid", "ipts"), None),
        P("ipts", "grid"),
        P("grid", "ipts"),
    )
    return jax.shard_map(
        local, mesh=mesh, in_specs=placed, out_specs=P(("grid", "ipts"), None), check_vma=False
    )
```

```python
import functools
import math

import jax
import jax.numpy as jnp
from jax import lax
from jax.experimental import pallas as pl
from jax.experimental.pallas import tpu as pltpu
from jax.sharding import PartitionSpec as P

MESH = pl.DeviceIdType.MESH
LANES = 128
WIDTH = 1024
SPLIT = 2
EARLY = (3, 8)
DIRECT = 1
LOANS = 16
ROOM, MOST = 8 << 20, 63 << 20
SORTS = ("index", "slab", "targets", "lent", "near", "early", "values", "target values", "sums")
F32, BF16 = jnp.float32, jnp.bfloat16


class Names:
    def __init__(self, size):
        self.size, self.known = size, ({}, {})

    def __getitem__(self, key):
        kind, name = key
        number = self.known[kind].setdefault(name, len(self.known[kind]))
        assert number < self.size
        return number


def kernel(groups, slabs, orbitals, targets, points, potential, out,
           slab, values, target_values, weights, lent, target_rows, index, hot, far_hot,
           early_out, early_near, early_in, near_out, near_in, leaving, arriving, crossing, kept, head,
           local_sem, send_sem, recv_sem, plane_send, plane_recv, partner_recv):
    g = lax.axis_index("grid")
    z = lax.axis_index("ipts")
    side = z // 2
    q = z + side * (groups - 1 - 2 * z)
    inward, outward = z + 1 - 2 * side, z - 1 + 2 * side
    rows, norb = orbitals.shape
    nj = targets.shape[1]
    count = points.shape[1]
    total = slabs * count
    lanes = slabs // 2
    lane, core = g // 2, lax.rem(g, 2)
    partner = g + 1 - 2 * core
    bits = [1 << n for n in range(lanes.bit_length() - 1)]
    orders = (bits, bits[::-1])
    early = norb * EARLY[0] // EARLY[1]
    tail = norb - early
    pieces = tail // LANES
    sub = rows // SPLIT
    quarter = sub // 2
    loan = rows // LOANS
    width = min(WIDTH, total)
    names = Names(recv_sem.shape[0])

    def where(block):
        return block + side * (groups - 1 - 2 * block)

    def cols(k):
        return pl.ds(k * LANES, LANES)

    last = pl.ds(tail, early)

    def place(slab_index):
        return pl.ds(pl.multiple_of(slab_index * count, count), count)

    def flipped(mask, of_core):
        there = lane
        for bit in bits:
            if mask & bit:
                there = there + bit - 2 * bit * lax.rem(lane // bit, 2)
        return 2 * there + of_core

    def send(kind, name, sort, src, dst, target):
        pltpu.make_async_remote_copy(
            src_ref=src, dst_ref=dst, send_sem=send_sem.at[SORTS.index(sort)], recv_sem=recv_sem.at[names[kind, name]],
            device_id={"grid": g, "ipts": target}, device_id_type=MESH).start()

    def receive(kind, name, dst):
        pltpu.make_async_copy(dst, dst, recv_sem.at[names[kind, name]]).wait()

    def left(sort, *views):
        for view in views:
            pltpu.make_async_copy(view, view, send_sem.at[SORTS.index(sort)]).wait()

    wide = pieces + 1
    direct = max(pieces - DIRECT, 1)

    def pass_to(block, item, way, target):
        recv = partner_recv.at[item // wide] if way is None else plane_recv.at[item, way]
        pltpu.make_async_remote_copy(
            src_ref=block, dst_ref=block, send_sem=plane_send.at[item // wide], recv_sem=recv,
            device_id={"grid": target, "ipts": z}, device_id_type=MESH).start()

    routed = [mask for mask in range(1, lanes) if mask not in bits]

    def way_of(mask, slot):
        if mask in bits:
            return bits.index(mask)
        return len(bits) + slot * len(routed) + routed.index(mask)

    def ways(mask, slots):
        if mask in bits:
            return [(way_of(mask, None), None)]
        return [(way_of(mask, slot), slot) for slot in range(slots)]

    def spread(item, view, slots):
        for bit in bits:
            pass_to(view(None, place(g)), item, way_of(bit, None), flipped(bit, core))
        pass_to(view(None, place(g)), item, None, partner)

    def spread_straight(item, view):
        for mask in range(1, lanes):
            pass_to(view(0, place(g)), item, way_of(mask, 0), flipped(mask, core))
        pass_to(view(0, place(g)), item, None, partner)

    def hand_over(item, view):
        for mask in range(1, lanes):
            block = view(0, place(flipped(mask, core)))
            pltpu.make_async_copy(block, block, plane_recv.at[item, way_of(mask, 0)]).wait()
            pass_to(block, item, None, partner)

    def forward(item, view, slots, single):
        masks = [m for m in range(1, lanes) if (m in bits) == single]
        for mask in sorted(masks, key=lambda m: m.bit_count()):
            for way, slot in ways(mask, slots):
                block = view(slot, place(flipped(mask, core)))
                pltpu.make_async_copy(block, block, plane_recv.at[item, way]).wait()
                for n in range(slots) if slot is None else (slot,):
                    order = orders[n]
                    top = max(order.index(bit) for bit in bits if mask & bit)
                    for bit in order[top + 1:]:
                        pass_to(view(n, place(flipped(mask, core))), item, way_of(mask | bit, n), flipped(bit, core))
                pass_to(block, item, None, partner)

    def all_of(blocks, pick):
        several = pl.ds(0, blocks * count)
        return (values.at[pick, several, :], target_values.at[pick, several, :])

    def gathered(pick):
        for n, view in enumerate(all_of(lanes, pick)):
            pltpu.make_async_copy(view, view, partner_recv.at[n]).wait()

    def passed(pick):
        for n, view in enumerate(all_of(slabs - 1, pick)):
            pltpu.make_async_copy(view, view, plane_send.at[n]).wait()

    def contribution(block, part, slot, kernel_rows):
        acc = None
        for start in range(0, total, width):
            some = pl.ds(start, width)
            products = lax.dot_general(
                slab[block, part, :], values[slot, some, :], (((1,), (1,)), ((), ())),
                preferred_element_type=F32)
            weighted = (kernel_rows[part, some].astype(F32) * products).astype(BF16)
            term = jnp.dot(weighted, target_values[slot, some, :], preferred_element_type=F32)
            acc = term if acc is None else acc + term
        return acc

    def begin(block, part):
        head[...] = lax.dot_general(
            slab[block, part, pl.ds(0, tail)], values[0, :, pl.ds(0, tail)], (((1,), (1,)), ((), ())),
            preferred_element_type=F32)

    def complete(block, part, kernel_rows):
        products = head[...] + lax.dot_general(
            slab[block, part, last], values[0, :, last], (((1,), (1,)), ((), ())), preferred_element_type=F32)
        weighted = (kernel_rows[part, :].astype(F32) * products).astype(BF16)
        return jnp.dot(weighted, target_values[0], preferred_element_type=F32)

    own_rows = pltpu.make_async_copy(orbitals, slab.at[q], local_sem.at[0])
    own_targets = pltpu.make_async_copy(targets, target_rows.at[q], local_sem.at[1])
    own_points = pltpu.make_async_copy(points, index.at[q], local_sem.at[2])
    own_weights = [
        pltpu.make_async_copy(
            potential.at[pl.ds(pl.multiple_of(where(block) * rows, rows), rows), :], weights.at[block],
            local_sem.at[3 + block])
        for block in range(groups)
    ]
    own_points.start()
    own_rows.start()
    own_targets.start()
    for copy in own_weights:
        copy.start()

    barrier = pltpu.get_barrier_semaphore()

    def greet(grid, group):
        pl.semaphore_signal(barrier, inc=1, device_id={"grid": grid, "ipts": group}, device_id_type=MESH)

    greet(g, inward)
    pl.when(q > 0)(lambda: greet(g, outward))
    greet(partner, z)
    for mask in range(1, lanes):
        if mask in bits:
            greet(flipped(mask, core), z)
        else:
            pl.when(q == 0)(lambda mask=mask: greet(flipped(mask, core), z))
    pl.semaphore_wait(barrier, jnp.where(q == 0, lanes + 1, len(bits) + 3))

    halves = range(SPLIT)

    quarters = [(2 * half, 2 * half + 1) for half in halves]

    def few(n):
        return pl.ds(n * quarter, quarter)

    def mark(ref, marked, blocks):
        spot = lax.broadcasted_iota(jnp.int32, (count, LANES), 1)
        for n, group in enumerate(marked):
            wanted = jnp.broadcast_to(index[group], (LANES, count)).T
            for m, block in enumerate(blocks):
                start = (g * groups + where(block)) * rows
                for c in range(rows // LANES):
                    chosen = (wanted == spot + (start + c * LANES)).astype(F32).astype(BF16)
                    ref[pl.ds(n * count, count), pl.ds(m * rows + c * LANES, LANES)] = chosen

    def pick(marks, blocks, rows_of):
        return sum(
            jnp.dot(marks[:, pl.ds(m * rows, rows)], rows_of(block), preferred_element_type=F32)
            for m, block in enumerate(blocks))

    def end():
        own_points.wait()
        send(1, "index", "index", index.at[0], index.at[0], inward)
        send(1, "early rows", "slab", orbitals.at[:, last], slab.at[0, :, last], inward)
        send(1, "targets", "targets", targets, target_rows.at[0], inward)
        for k in range(pieces):
            send(1, ("end", k), "slab", orbitals.at[:, cols(k)], slab.at[0, :, cols(k)], inward)

        def lend(n):
            part = pl.ds(pl.multiple_of(where(1) * rows + n * loan, loan), loan)
            send(1, ("lent", n * SPLIT // LOANS), "lent", potential.at[part, :], lent.at[pl.ds(n * loan, loan), :], inward)

        for n in range(LOANS - 2):
            lend(n)
        views = [lambda n, p: values.at[0, p, last]]
        views += [lambda n, p, k=k: values.at[0, p, cols(k)] for k in range(pieces)]
        views += [lambda n, p: target_values.at[0, p, :]]
        marks = hot.at[pl.ds(0, count), :]
        mark(marks, (0,), (0, 2, 3))
        own_rows.wait()
        receive(0, "near", near_in)
        for item in (0, wide):
            receive(0, ("value", item), views[item](0, place(g)))
            spread_straight(item, views[item])
        waiting = [0, wide]
        for k in range(pieces):
            if k < direct:
                for block in (2, 3):
                    receive(0, ("out", block, k), slab.at[block, :, cols(k)])
                found = pick(marks, (0, 2, 3), lambda block: slab[block, :, cols(k)])
                values[0, place(g), cols(k)] = (found + near_in[:, cols(k)].astype(F32)).astype(BF16)
            else:
                receive(0, ("value", k + 1), views[k + 1](0, place(g)))
            spread_straight(k + 1, views[k + 1])
            while len(waiting) > 1:
                item = waiting.pop(0)
                hand_over(item, views[item])
            waiting.append(k + 1)
        for item in waiting:
            hand_over(item, views[item])
        own_targets.wait()
        for copy in own_weights:
            copy.wait()
        gathered(0)
        for k in range(direct, pieces):
            for block in (2, 3):
                receive(0, ("out", block, k), slab.at[block, :, cols(k)])
        begin(3, few(0))
        for block in (3, 2):
            for n in range(2 * SPLIT):
                receive(0, ("out rows", block, n), slab.at[block, few(n), last])
                leaving[block - 2, few(n), :] = complete(block, few(n), weights.at[block]).astype(BF16)
                send(1, ("sum", block, n), "sums", leaving.at[block - 2, few(n), :],
                     arriving.at[block - 2, few(n), :], inward)
                if n + 1 < 2 * SPLIT:
                    begin(block, few(n + 1))
                elif block == 3:
                    begin(2, few(0))
                if block == 2 and n == SPLIT - 1:
                    lend(LOANS - 2)
        lend(LOANS - 1)
        for half in halves:
            part = pl.ds(half * sub, sub)
            kept[0, part, :] = contribution(0, part, 0, weights.at[0])
        for n in range(2 * SPLIT):
            receive(0, ("end sum", n), arriving.at[0, few(n), :])
            out[few(n), :] = (-(kept[0, few(n), :] + arriving[0, few(n), :].astype(F32))).astype(out.dtype)
        left("index", index.at[0])
        left("slab", slab.at[0])
        left("targets", target_rows.at[0])
        left("lent", lent)
        left("sums", leaving.at[pl.ds(0, 2)])
        passed(0)

    def inner():
        both = pl.ds(0, 2)
        own_points.wait()
        send(1, "index in", "index", index.at[1], index.at[2], inward)

        def own(k):
            send(1, ("own", k), "slab", orbitals.at[:, cols(k)], slab.at[2, :, cols(k)], inward)

        first = min(pieces, 3)
        for k in range(first):
            own(k)
        receive(1, "index", index.at[0])
        send(1, "index end", "index", index.at[0], index.at[3], inward)
        for k in range(first, pieces):
            own(k)

        def relay(block, k):
            send(0, ("out", block, k), "slab", slab.at[block, :, cols(k)], slab.at[block, :, cols(k)], outward)

        def relay_own(k):
            receive(1, ("own", k), slab.at[2, :, cols(k)])
            relay(2, k)

        def cross(k):
            receive(1, ("end", k), slab.at[0, :, cols(k)])
            send(1, ("end in", k), "slab", slab.at[0, :, cols(k)], slab.at[3, :, cols(k)], inward)

        mark(hot, (1, 0), range(groups))
        own_rows.wait()
        near_out[...] = jnp.dot(
            hot[pl.ds(count, count), pl.ds(rows, rows)], slab[1, :, pl.ds(0, direct * LANES)],
            preferred_element_type=F32).astype(BF16)
        send(0, "near", "near", near_out, near_in, outward)
        ahead = max(pieces - 2, 0)
        for k in range(ahead):
            relay_own(k)
        receive(1, "index in", index.at[2])
        receive(1, "index end", index.at[3])
        mark(far_hot, (2, 3), (0, 1))
        own_targets.wait()
        receive(1, "early rows", slab.at[0, :, last])
        orbital_part, target_part = pl.ds(0, early), pl.ds(early, nj)
        early_out[:, orbital_part] = pick(far_hot, (0, 1), lambda b: slab[b, :, last]).astype(BF16)
        send(1, "early", "early", early_out.at[:, orbital_part], early_in.at[:, orbital_part], inward)
        early_near[:, orbital_part] = pick(hot, (0, 1), lambda b: slab[b, :, last]).astype(BF16)
        for k in range(ahead, pieces):
            relay_own(k)
        receive(1, "targets", target_rows.at[0])
        early_out[:, target_part] = pick(far_hot, (0, 1), lambda b: target_rows[b]).astype(BF16)
        send(1, "early targets", "early", early_out.at[:, target_part], early_in.at[:, target_part], inward)
        early_near[:, target_part] = pick(hot, (0, 1), lambda b: target_rows[b]).astype(BF16)
        ready = 1
        cross(0)

        views = [lambda n, p: values.at[both if n is None else n, p, last]]
        views += [lambda n, p, k=k: values.at[both if n is None else n, p, cols(k)] for k in range(pieces)]
        views += [lambda n, p: target_values.at[both if n is None else n, p, :]]

        def found_early(part):
            return early_near[:, part].astype(F32) + early_in[:, part].astype(F32)

        receive(1, "early", early_in.at[:, orbital_part])
        found = found_early(orbital_part)
        for n in range(2):
            values[n, place(g), last] = found[n * count:(n + 1) * count].astype(BF16)
        send(0, ("value", 0), "values", values.at[1, place(g), last], values.at[0, place(g), last], outward)
        spread(0, views[0], 2)
        if pieces > 1:
            ready = 2
            cross(1)
        receive(1, "early targets", early_in.at[:, target_part])
        found = found_early(target_part)
        for n in range(2):
            target_values[n, place(g), :] = found[n * count:(n + 1) * count].astype(BF16)
        send(0, ("value", wide), "target values", target_values.at[1, place(g), :],
             target_values.at[0, place(g), :], outward)
        spread(wide, views[wide], 2)

        def rows_in():
            for block in (0, 1):
                for n in range(2 * SPLIT):
                    send(1, ("rows in", 3 - block, n), "slab", slab.at[block, few(n), last],
                         slab.at[3 - block, few(n), last], inward)

        batches = [[0, wide]] + [[k + 1] for k in range(pieces)]

        def onward(n, single):
            for item in batches[n]:
                forward(item, views[item], 2, single)

        for k in range(pieces):
            while ready < min(pieces, 3 + k):
                cross(ready)
                ready += 1
                if ready == pieces:
                    rows_in()
            receive(1, ("end in", k), slab.at[3, :, cols(k)])
            if k < direct:
                relay(3, k)
            found = pick(hot, range(groups), lambda b: slab[b, :, cols(k)])
            for n in range(2):
                values[n, place(g), cols(k)] = found[n * count:(n + 1) * count].astype(BF16)
            if k >= direct:
                send(0, ("value", k + 1), "values", values.at[1, place(g), cols(k)],
                     values.at[0, place(g), cols(k)], outward)
                relay(3, k)
            spread(k + 1, views[k + 1], 2)
            if k > 0:
                onward(k - 1, True)
            if k > 2:
                onward(k - 3, False)

        def pass_on(block, n):
            receive(1, ("rows in", block, n), slab.at[block, few(n), last])
            send(0, ("out rows", block, n), "slab", slab.at[block, few(n), last],
                 slab.at[block, few(n), last], outward)

        def keep(block, half, slot, kernel_rows):
            part = pl.ds(half * sub, sub)
            kept[block, part, :] = contribution(block, part, slot, kernel_rows)

        def sums(block, half):
            for n in quarters[half]:
                receive(1, ("sum", block, n), arriving.at[block - 2, few(n), :])
                leaving[block - 2, few(n), :] = (
                    kept[block, few(n), :] + arriving[block - 2, few(n), :].astype(F32)).astype(BF16)
                send(1, ("sum in", block, n), "sums", leaving.at[block - 2, few(n), :],
                     crossing.at[3 - block, few(n), :], inward)

        def end_sums(half):
            for n in quarters[half]:
                receive(1, ("sum in", 3, n), crossing.at[0, few(n), :])
                leaving[2, few(n), :] = (kept[0, few(n), :] + crossing[0, few(n), :].astype(F32)).astype(BF16)
                send(0, ("end sum", n), "sums", leaving.at[2, few(n), :], arriving.at[0, few(n), :], outward)

        def near(half):
            part = pl.ds(half * sub, sub)
            keep(1, half, 0, weights.at[1])
            receive(1, ("lent", half), lent.at[part, :])
            kept[1, part, :] += contribution(1, part, 1, lent)

        pass_on(3, 0)
        onward(pieces - 1, True)
        for n in range(max(pieces - 3, 0), pieces - 2):
            onward(n, False)
        pass_on(3, 1)
        onward(pieces - 2, False)
        onward(pieces, True)
        pass_on(3, 2)
        onward(pieces - 1, False)
        onward(pieces, False)
        for copy in own_weights:
            copy.wait()
        gathered(both)
        keep(3, 0, 0, weights.at[3])
        pass_on(3, 3)
        keep(3, 1, 0, weights.at[3])
        pass_on(2, 0)
        keep(0, 0, 0, weights.at[0])
        pass_on(2, 1)
        keep(2, 0, 0, weights.at[2])
        pass_on(2, 2)
        sums(3, 0)
        pass_on(2, 3)
        keep(2, 1, 0, weights.at[2])
        keep(0, 1, 0, weights.at[0])
        sums(3, 1)
        end_sums(0)
        sums(2, 0)
        end_sums(1)
        near(0)
        sums(2, 1)
        near(1)
        for n in range(2 * SPLIT):
            receive(1, ("sum in", 2, n), crossing.at[1, few(n), :])
            out[few(n), :] = (-(kept[1, few(n), :] + crossing[1, few(n), :].astype(F32))).astype(out.dtype)
        left("index", index.at[both])
        left("slab", slab)
        left("near", near_out)
        left("early", early_out)
        left("values", values.at[0, pl.ds(0, count), pl.ds(direct * LANES, norb - direct * LANES)])
        left("target values", target_values.at[0, pl.ds(0, count), :])
        left("sums", leaving)
        passed(both)

    pl.when(q == 0)(end)
    pl.when(q == 1)(inner)


def local(orbitals, targets, points, potential):
    groups, slabs = lax.axis_size("ipts"), lax.axis_size("grid")
    assert groups == 4 and slabs.bit_count() == 1
    rows, norb = orbitals.shape
    nj = targets.shape[1]
    count = points.shape[1]
    early = norb * EARLY[0] // EARLY[1]
    pieces = (norb - early) // LANES
    transfers = 7 + 3 * pieces + 13 * SPLIT
    lanes = slabs // 2
    doublings = lanes.bit_length() - 1
    dma = pltpu.SemaphoreType.DMA
    buffers = [
        pltpu.VMEM((groups, rows, norb), BF16),
        pltpu.VMEM((2, slabs * count, norb), BF16),
        pltpu.VMEM((2, slabs * count, nj), BF16),
        pltpu.VMEM((groups, rows, slabs * count), BF16),
        pltpu.VMEM((rows, slabs * count), BF16),
        pltpu.VMEM((2, rows, nj), BF16),
        pltpu.VMEM((groups, 1, count), jnp.int32),
        pltpu.VMEM((2 * count, groups * rows), BF16),
        pltpu.VMEM((2 * count, 2 * rows), BF16),
        pltpu.VMEM((2 * count, early + nj), BF16),
        pltpu.VMEM((2 * count, early + nj), BF16),
        pltpu.VMEM((2 * count, early + nj), BF16),
        pltpu.VMEM((count, max(pieces - DIRECT, 1) * LANES), BF16),
        pltpu.VMEM((count, max(pieces - DIRECT, 1) * LANES), BF16),
        pltpu.VMEM((3, rows, nj), BF16),
        pltpu.VMEM((2, rows, nj), BF16),
        pltpu.VMEM((2, rows, nj), BF16),
        pltpu.VMEM((groups, rows, nj), F32),
        pltpu.VMEM((rows // (2 * SPLIT), slabs * count), F32),
    ]
    size = sum(math.prod(b.shape) * jnp.dtype(b.dtype).itemsize for b in buffers)
    limit = min(size + ROOM, MOST)
    held = [pltpu.with_memory_space_constraint(x, pltpu.HBM) for x in (orbitals, targets, points, potential)]
    return pl.pallas_call(
        functools.partial(kernel, groups, slabs),
        out_shape=jax.ShapeDtypeStruct((rows, nj), BF16),
        in_specs=[pl.BlockSpec(memory_space=pl.ANY)] * 4,
        out_specs=pl.BlockSpec(memory_space=pltpu.VMEM),
        scratch_shapes=buffers + [
            dma((3 + groups,)),
            dma((len(SORTS),)),
            dma((transfers,)),
            dma((2,)),
            dma((pieces + 2, doublings + 2 * (lanes - 1 - doublings))),
            dma((2,)),
        ],
        compiler_params=pltpu.CompilerParams(
            collective_id=0, has_side_effects=True, vmem_limit_bytes=limit),
    )(*held)


def solution(mesh):
    placed = (
        P(("grid", "ipts"), None),
        P(("grid", "ipts"), None),
        P("ipts", "grid"),
        P("grid", "ipts"),
    )
    return jax.shard_map(
        local, mesh=mesh, in_specs=placed, out_specs=P(("grid", "ipts"), None), check_vma=False
    )
```

```python
import functools
import math

import jax
import jax.numpy as jnp
from jax import lax
from jax.experimental import pallas as pl
from jax.experimental.pallas import tpu as pltpu
from jax.sharding import PartitionSpec as P

MESH = pl.DeviceIdType.MESH
LANES = 128
WIDTH = 1024
SPLIT = 2
EARLY = (3, 8)
DIRECT = 1
LOANS = 16
ROOM, MOST = 8 << 20, 63 << 20
SORTS = ("index", "slab", "targets", "lent", "near", "early", "values", "target values", "sums")
F32, BF16 = jnp.float32, jnp.bfloat16


class Names:
    def __init__(self, size):
        self.size, self.known = size, ({}, {})

    def __getitem__(self, key):
        kind, name = key
        number = self.known[kind].setdefault(name, len(self.known[kind]))
        assert number < self.size
        return number


def kernel(groups, slabs, orbitals, targets, points, potential, out,
           slab, values, target_values, weights, lent, target_rows, index, hot, far_hot,
           early_out, early_near, early_in, near_out, near_in, leaving, arriving, crossing, kept, head,
           local_sem, send_sem, recv_sem, plane_send, plane_recv, partner_recv):
    g = lax.axis_index("grid")
    z = lax.axis_index("ipts")
    side = z // 2
    q = z + side * (groups - 1 - 2 * z)
    inward, outward = z + 1 - 2 * side, z - 1 + 2 * side
    rows, norb = orbitals.shape
    nj = targets.shape[1]
    count = points.shape[1]
    total = slabs * count
    lanes = slabs // 2
    lane, core = g // 2, lax.rem(g, 2)
    partner = g + 1 - 2 * core
    bits = [1 << n for n in range(lanes.bit_length() - 1)]
    orders = (bits, bits[::-1])
    early = norb * EARLY[0] // EARLY[1]
    tail = norb - early
    pieces = tail // LANES
    sub = rows // SPLIT
    quarter = sub // 2
    loan = rows // LOANS
    width = min(WIDTH, total)
    names = Names(recv_sem.shape[0])

    def where(block):
        return block + side * (groups - 1 - 2 * block)

    def cols(k):
        return pl.ds(k * LANES, LANES)

    last = pl.ds(tail, early)

    def place(slab_index):
        return pl.ds(pl.multiple_of(slab_index * count, count), count)

    def flipped(mask, of_core):
        there = lane
        for bit in bits:
            if mask & bit:
                there = there + bit - 2 * bit * lax.rem(lane // bit, 2)
        return 2 * there + of_core

    def send(kind, name, sort, src, dst, target):
        pltpu.make_async_remote_copy(
            src_ref=src, dst_ref=dst, send_sem=send_sem.at[SORTS.index(sort)], recv_sem=recv_sem.at[names[kind, name]],
            device_id={"grid": g, "ipts": target}, device_id_type=MESH).start()

    def receive(kind, name, dst):
        pltpu.make_async_copy(dst, dst, recv_sem.at[names[kind, name]]).wait()

    def left(sort, *views):
        for view in views:
            pltpu.make_async_copy(view, view, send_sem.at[SORTS.index(sort)]).wait()

    wide = pieces + 1
    direct = max(pieces - DIRECT, 1)

    def pass_to(block, item, way, target):
        recv = partner_recv.at[item // wide] if way is None else plane_recv.at[item, way]
        pltpu.make_async_remote_copy(
            src_ref=block, dst_ref=block, send_sem=plane_send.at[item // wide], recv_sem=recv,
            device_id={"grid": target, "ipts": z}, device_id_type=MESH).start()

    routed = [mask for mask in range(1, lanes) if mask not in bits]

    def way_of(mask, slot):
        if mask in bits:
            return bits.index(mask)
        return len(bits) + slot * len(routed) + routed.index(mask)

    def ways(mask, slots):
        if mask in bits:
            return [(way_of(mask, None), None)]
        return [(way_of(mask, slot), slot) for slot in range(slots)]

    def spread(item, view, slots):
        for bit in bits:
            pass_to(view(None, place(g)), item, way_of(bit, None), flipped(bit, core))
        pass_to(view(None, place(g)), item, None, partner)

    def spread_straight(item, view):
        for mask in range(1, lanes):
            pass_to(view(0, place(g)), item, way_of(mask, 0), flipped(mask, core))
        pass_to(view(0, place(g)), item, None, partner)

    def hand_over(item, view):
        for mask in range(1, lanes):
            block = view(0, place(flipped(mask, core)))
            pltpu.make_async_copy(block, block, plane_recv.at[item, way_of(mask, 0)]).wait()
            pass_to(block, item, None, partner)

    def forward(item, view, slots, single):
        masks = [m for m in range(1, lanes) if (m in bits) == single]
        for mask in sorted(masks, key=lambda m: m.bit_count()):
            for way, slot in ways(mask, slots):
                block = view(slot, place(flipped(mask, core)))
                pltpu.make_async_copy(block, block, plane_recv.at[item, way]).wait()
                for n in range(slots) if slot is None else (slot,):
                    order = orders[n]
                    top = max(order.index(bit) for bit in bits if mask & bit)
                    for bit in order[top + 1:]:
                        pass_to(view(n, place(flipped(mask, core))), item, way_of(mask | bit, n), flipped(bit, core))
                pass_to(block, item, None, partner)

    def all_of(blocks, pick):
        several = pl.ds(0, blocks * count)
        return (values.at[pick, several, :], target_values.at[pick, several, :])

    def gathered(pick):
        for n, view in enumerate(all_of(lanes, pick)):
            pltpu.make_async_copy(view, view, partner_recv.at[n]).wait()

    def passed(pick):
        for n, view in enumerate(all_of(slabs - 1, pick)):
            pltpu.make_async_copy(view, view, plane_send.at[n]).wait()

    def contribution(block, part, slot, kernel_rows):
        acc = None
        for start in range(0, total, width):
            some = pl.ds(start, width)
            products = lax.dot_general(
                slab[block, part, :], values[slot, some, :], (((1,), (1,)), ((), ())),
                preferred_element_type=F32)
            weighted = (kernel_rows[part, some].astype(F32) * products).astype(BF16)
            term = jnp.dot(weighted, target_values[slot, some, :], preferred_element_type=F32)
            acc = term if acc is None else acc + term
        return acc

    def begin(block, part):
        head[...] = lax.dot_general(
            slab[block, part, pl.ds(0, tail)], values[0, :, pl.ds(0, tail)], (((1,), (1,)), ((), ())),
            preferred_element_type=F32)

    def complete(block, part, kernel_rows):
        products = head[...] + lax.dot_general(
            slab[block, part, last], values[0, :, last], (((1,), (1,)), ((), ())), preferred_element_type=F32)
        weighted = (kernel_rows[part, :].astype(F32) * products).astype(BF16)
        return jnp.dot(weighted, target_values[0], preferred_element_type=F32)

    own_rows = pltpu.make_async_copy(orbitals, slab.at[q], local_sem.at[0])
    own_targets = pltpu.make_async_copy(targets, target_rows.at[q], local_sem.at[1])
    own_points = pltpu.make_async_copy(points, index.at[q], local_sem.at[2])
    own_weights = [
        pltpu.make_async_copy(
            potential.at[pl.ds(pl.multiple_of(where(block) * rows, rows), rows), :], weights.at[block],
            local_sem.at[3])
        for block in range(groups)
    ]
    own_points.start()
    own_rows.start()
    own_targets.start()
    for copy in own_weights:
        copy.start()

    barrier = pltpu.get_barrier_semaphore()

    def greet(grid, group):
        pl.semaphore_signal(barrier, inc=1, device_id={"grid": grid, "ipts": group}, device_id_type=MESH)

    greet(g, inward)
    pl.when(q > 0)(lambda: greet(g, outward))
    greet(partner, z)
    for mask in range(1, lanes):
        if mask in bits:
            greet(flipped(mask, core), z)
        else:
            pl.when(q == 0)(lambda mask=mask: greet(flipped(mask, core), z))
    pl.semaphore_wait(barrier, jnp.where(q == 0, lanes + 1, len(bits) + 3))

    halves = range(SPLIT)

    quarters = [(2 * half, 2 * half + 1) for half in halves]

    def few(n):
        return pl.ds(n * quarter, quarter)

    def parts(block, n):
        if block == 2 and n == 2 * SPLIT - 1:
            return [pl.ds(n * quarter + m * (quarter // 2), quarter // 2) for m in range(2)]
        return [few(n)]

    def mark(ref, marked, blocks):
        spot = lax.broadcasted_iota(jnp.int32, (count, LANES), 1)
        for n, group in enumerate(marked):
            wanted = jnp.broadcast_to(index[group], (LANES, count)).T
            for m, block in enumerate(blocks):
                start = (g * groups + where(block)) * rows
                for c in range(rows // LANES):
                    chosen = (wanted == spot + (start + c * LANES)).astype(F32).astype(BF16)
                    ref[pl.ds(n * count, count), pl.ds(m * rows + c * LANES, LANES)] = chosen

    def pick(marks, blocks, rows_of):
        return sum(
            jnp.dot(marks[:, pl.ds(m * rows, rows)], rows_of(block), preferred_element_type=F32)
            for m, block in enumerate(blocks))

    def end():
        own_points.wait()
        send(1, "index", "index", index.at[0], index.at[0], inward)
        own_rows.wait()
        send(1, "early rows", "slab", slab.at[0, :, last], slab.at[0, :, last], inward)
        send(1, "targets", "targets", targets, target_rows.at[0], inward)
        for k in range(pieces):
            send(1, ("end", k), "slab", slab.at[0, :, cols(k)], slab.at[0, :, cols(k)], inward)

        def lend(n):
            part = pl.ds(pl.multiple_of(where(1) * rows + n * loan, loan), loan)
            send(1, ("lent", n * SPLIT // LOANS), "lent", potential.at[part, :], lent.at[pl.ds(n * loan, loan), :], inward)

        for n in range(LOANS - 2):
            lend(n)
        views = [lambda n, p: values.at[0, p, last]]
        views += [lambda n, p, k=k: values.at[0, p, cols(k)] for k in range(pieces)]
        views += [lambda n, p: target_values.at[0, p, :]]
        marks = hot.at[pl.ds(0, count), :]
        mark(marks, (0,), (0, 2, 3))
        receive(0, "near", near_in)
        for item in (0, wide):
            receive(0, ("value", item), views[item](0, place(g)))
            spread_straight(item, views[item])
        waiting = [0, wide]
        for k in range(pieces):
            if k < direct:
                for block in (2, 3):
                    receive(0, ("out", block, k), slab.at[block, :, cols(k)])
                found = pick(marks, (0, 2, 3), lambda block: slab[block, :, cols(k)])
                values[0, place(g), cols(k)] = (found + near_in[:, cols(k)].astype(F32)).astype(BF16)
            else:
                receive(0, ("value", k + 1), views[k + 1](0, place(g)))
            spread_straight(k + 1, views[k + 1])
            while len(waiting) > 1:
                item = waiting.pop(0)
                hand_over(item, views[item])
            waiting.append(k + 1)
        for item in waiting:
            hand_over(item, views[item])
        own_targets.wait()
        pltpu.make_async_copy(weights, weights, local_sem.at[3]).wait()
        gathered(0)
        for k in range(direct, pieces):
            for block in (2, 3):
                receive(0, ("out", block, k), slab.at[block, :, cols(k)])
        begin(3, few(0))
        for block in (3, 2):
            for n in range(2 * SPLIT):
                receive(0, ("out rows", block, n), slab.at[block, few(n), last])
                leaving[block - 2, few(n), :] = complete(block, few(n), weights.at[block]).astype(BF16)
                for part in parts(block, n):
                    send(1, ("sum", block, part.start), "sums", leaving.at[block - 2, part, :],
                         arriving.at[block - 2, part, :], inward)
                if n + 1 < 2 * SPLIT:
                    begin(block, few(n + 1))
                elif block == 3:
                    begin(2, few(0))
                if block == 2 and n == SPLIT - 1:
                    lend(LOANS - 2)
        lend(LOANS - 1)
        for half in halves:
            part = pl.ds(half * sub, sub)
            kept[0, part, :] = contribution(0, part, 0, weights.at[0])
        for n in range(2 * SPLIT):
            receive(0, ("end sum", n), arriving.at[0, few(n), :])
            out[few(n), :] = (-(kept[0, few(n), :] + arriving[0, few(n), :].astype(F32))).astype(out.dtype)
        left("index", index.at[0])
        left("slab", slab.at[0])
        left("targets", target_rows.at[0])
        left("lent", lent)
        left("sums", leaving.at[pl.ds(0, 2)])
        passed(0)

    def inner():
        both = pl.ds(0, 2)
        own_points.wait()
        send(1, "index in", "index", index.at[1], index.at[2], inward)

        def own(k):
            send(1, ("own", k), "slab", slab.at[1, :, cols(k)], slab.at[2, :, cols(k)], inward)

        own_rows.wait()
        first = min(pieces, 3)
        for k in range(first):
            own(k)
        receive(1, "index", index.at[0])
        send(1, "index in", "index", index.at[0], index.at[3], inward)
        for k in range(first, pieces):
            own(k)

        def relay(block, k):
            send(0, ("out", block, k), "slab", slab.at[block, :, cols(k)], slab.at[block, :, cols(k)], outward)

        def relay_own(k):
            receive(1, ("own", k), slab.at[2, :, cols(k)])
            relay(2, k)

        def cross(k):
            receive(1, ("end", k), slab.at[0, :, cols(k)])
            send(1, ("end in", k), "slab", slab.at[0, :, cols(k)], slab.at[3, :, cols(k)], inward)

        mark(hot, (1, 0), range(groups))
        near_out[...] = jnp.dot(
            hot[pl.ds(count, count), pl.ds(rows, rows)], slab[1, :, pl.ds(0, direct * LANES)],
            preferred_element_type=F32).astype(BF16)
        send(0, "near", "near", near_out, near_in, outward)
        ahead = max(pieces - 2, 0)
        for k in range(ahead):
            relay_own(k)
        receive(1, "index in", index.at[pl.ds(2, 2)])
        mark(far_hot, (2, 3), (0, 1))
        own_targets.wait()
        receive(1, "early rows", slab.at[0, :, last])
        orbital_part, target_part = pl.ds(0, early), pl.ds(early, nj)
        early_out[:, orbital_part] = pick(far_hot, (0, 1), lambda b: slab[b, :, last]).astype(BF16)
        send(1, "early", "early", early_out.at[:, orbital_part], early_in.at[:, orbital_part], inward)
        early_near[:, orbital_part] = pick(hot, (0, 1), lambda b: slab[b, :, last]).astype(BF16)
        for k in range(ahead, pieces):
            relay_own(k)
        receive(1, "targets", target_rows.at[0])
        early_out[:, target_part] = pick(far_hot, (0, 1), lambda b: target_rows[b]).astype(BF16)
        send(1, "early targets", "early", early_out.at[:, target_part], early_in.at[:, target_part], inward)
        early_near[:, target_part] = pick(hot, (0, 1), lambda b: target_rows[b]).astype(BF16)
        ready = 1
        cross(0)

        views = [lambda n, p: values.at[both if n is None else n, p, last]]
        views += [lambda n, p, k=k: values.at[both if n is None else n, p, cols(k)] for k in range(pieces)]
        views += [lambda n, p: target_values.at[both if n is None else n, p, :]]

        def found_early(part):
            return early_near[:, part].astype(F32) + early_in[:, part].astype(F32)

        receive(1, "early", early_in.at[:, orbital_part])
        found = found_early(orbital_part)
        for n in range(2):
            values[n, place(g), last] = found[n * count:(n + 1) * count].astype(BF16)
        send(0, ("value", 0), "values", values.at[1, place(g), last], values.at[0, place(g), last], outward)
        spread(0, views[0], 2)
        if pieces > 1:
            ready = 2
            cross(1)
        receive(1, "early targets", early_in.at[:, target_part])
        found = found_early(target_part)
        for n in range(2):
            target_values[n, place(g), :] = found[n * count:(n + 1) * count].astype(BF16)
        send(0, ("value", wide), "target values", target_values.at[1, place(g), :],
             target_values.at[0, place(g), :], outward)
        spread(wide, views[wide], 2)

        def rows_in():
            for block in (0, 1):
                for n in range(2 * SPLIT):
                    send(1, ("rows in", 3 - block, n), "slab", slab.at[block, few(n), last],
                         slab.at[3 - block, few(n), last], inward)

        batches = [[0, wide]] + [[k + 1] for k in range(pieces)]

        def onward(n, single):
            for item in batches[n]:
                forward(item, views[item], 2, single)

        for k in range(pieces):
            while ready < min(pieces, 3 + k):
                cross(ready)
                ready += 1
                if ready == pieces:
                    rows_in()
            receive(1, ("end in", k), slab.at[3, :, cols(k)])
            if k < direct:
                relay(3, k)
            found = pick(hot, range(groups), lambda b: slab[b, :, cols(k)])
            for n in range(2):
                values[n, place(g), cols(k)] = found[n * count:(n + 1) * count].astype(BF16)
            if k >= direct:
                send(0, ("value", k + 1), "values", values.at[1, place(g), cols(k)],
                     values.at[0, place(g), cols(k)], outward)
                relay(3, k)
            spread(k + 1, views[k + 1], 2)
            if k > 0:
                onward(k - 1, True)
            if k > 2:
                onward(k - 3, False)

        def pass_on(block, n):
            receive(1, ("rows in", block, n), slab.at[block, few(n), last])
            send(0, ("out rows", block, n), "slab", slab.at[block, few(n), last],
                 slab.at[block, few(n), last], outward)

        def keep(block, half, slot, kernel_rows):
            part = pl.ds(half * sub, sub)
            kept[block, part, :] = contribution(block, part, slot, kernel_rows)

        def sums(block, half):
            for n in quarters[half]:
                for part in parts(block, n):
                    receive(1, ("sum", block, part.start), arriving.at[block - 2, part, :])
                    leaving[block - 2, part, :] = (
                        kept[block, part, :] + arriving[block - 2, part, :].astype(F32)).astype(BF16)
                    send(1, ("sum in", block, part.start), "sums", leaving.at[block - 2, part, :],
                         crossing.at[3 - block, part, :], inward)

        def end_sums(half):
            for n in quarters[half]:
                receive(1, ("sum in", 3, few(n).start), crossing.at[0, few(n), :])
                leaving[2, few(n), :] = (kept[0, few(n), :] + crossing[0, few(n), :].astype(F32)).astype(BF16)
                send(0, ("end sum", n), "sums", leaving.at[2, few(n), :], arriving.at[0, few(n), :], outward)

        def near(half):
            part = pl.ds(half * sub, sub)
            keep(1, half, 0, weights.at[1])
            receive(1, ("lent", half), lent.at[part, :])
            kept[1, part, :] += contribution(1, part, 1, lent)

        pass_on(3, 0)
        onward(pieces - 1, True)
        for n in range(max(pieces - 3, 0), pieces - 2):
            onward(n, False)
        pass_on(3, 1)
        onward(pieces - 2, False)
        onward(pieces, True)
        pass_on(3, 2)
        onward(pieces - 1, False)
        onward(pieces, False)
        pltpu.make_async_copy(weights, weights, local_sem.at[3]).wait()
        gathered(both)
        keep(3, 0, 0, weights.at[3])
        pass_on(3, 3)
        keep(3, 1, 0, weights.at[3])
        pass_on(2, 0)
        keep(0, 0, 0, weights.at[0])
        pass_on(2, 1)
        keep(2, 0, 0, weights.at[2])
        pass_on(2, 2)
        sums(3, 0)
        pass_on(2, 3)
        keep(2, 1, 0, weights.at[2])
        keep(0, 1, 0, weights.at[0])
        sums(3, 1)
        end_sums(0)
        sums(2, 0)
        end_sums(1)
        near(0)
        sums(2, 1)
        near(1)
        for n in range(2 * SPLIT):
            for part in parts(2, n):
                receive(1, ("sum in", 2, part.start), crossing.at[1, part, :])
                out[part, :] = (-(kept[1, part, :] + crossing[1, part, :].astype(F32))).astype(out.dtype)
        left("index", index.at[both])
        left("slab", slab)
        left("near", near_out)
        left("early", early_out)
        left("values", values.at[0, pl.ds(0, count), pl.ds(direct * LANES, norb - direct * LANES)])
        left("target values", target_values.at[0, pl.ds(0, count), :])
        left("sums", leaving)
        passed(both)

    pl.when(q == 0)(end)
    pl.when(q == 1)(inner)


def local(orbitals, targets, points, potential):
    groups, slabs = lax.axis_size("ipts"), lax.axis_size("grid")
    assert groups == 4 and slabs.bit_count() == 1
    rows, norb = orbitals.shape
    nj = targets.shape[1]
    count = points.shape[1]
    early = norb * EARLY[0] // EARLY[1]
    pieces = (norb - early) // LANES
    transfers = 7 + 3 * pieces + 13 * SPLIT + 1
    lanes = slabs // 2
    doublings = lanes.bit_length() - 1
    dma = pltpu.SemaphoreType.DMA
    buffers = [
        pltpu.VMEM((groups, rows, norb), BF16),
        pltpu.VMEM((2, slabs * count, norb), BF16),
        pltpu.VMEM((2, slabs * count, nj), BF16),
        pltpu.VMEM((groups, rows, slabs * count), BF16),
        pltpu.VMEM((rows, slabs * count), BF16),
        pltpu.VMEM((2, rows, nj), BF16),
        pltpu.VMEM((groups, 1, count), jnp.int32),
        pltpu.VMEM((2 * count, groups * rows), BF16),
        pltpu.VMEM((2 * count, 2 * rows), BF16),
        pltpu.VMEM((2 * count, early + nj), BF16),
        pltpu.VMEM((2 * count, early + nj), BF16),
        pltpu.VMEM((2 * count, early + nj), BF16),
        pltpu.VMEM((count, max(pieces - DIRECT, 1) * LANES), BF16),
        pltpu.VMEM((count, max(pieces - DIRECT, 1) * LANES), BF16),
        pltpu.VMEM((3, rows, nj), BF16),
        pltpu.VMEM((2, rows, nj), BF16),
        pltpu.VMEM((2, rows, nj), BF16),
        pltpu.VMEM((groups, rows, nj), F32),
        pltpu.VMEM((rows // (2 * SPLIT), slabs * count), F32),
    ]
    size = sum(math.prod(b.shape) * jnp.dtype(b.dtype).itemsize for b in buffers)
    limit = min(size + ROOM, MOST)
    held = [pltpu.with_memory_space_constraint(x, pltpu.HBM) for x in (orbitals, targets, points, potential)]
    return pl.pallas_call(
        functools.partial(kernel, groups, slabs),
        out_shape=jax.ShapeDtypeStruct((rows, nj), BF16),
        in_specs=[pl.BlockSpec(memory_space=pl.ANY)] * 4,
        out_specs=pl.BlockSpec(memory_space=pltpu.VMEM),
        scratch_shapes=buffers + [
            dma((4,)),
            dma((len(SORTS),)),
            dma((transfers,)),
            dma((2,)),
            dma((pieces + 2, doublings + 2 * (lanes - 1 - doublings))),
            dma((2,)),
        ],
        compiler_params=pltpu.CompilerParams(
            collective_id=0, has_side_effects=True, vmem_limit_bytes=limit),
    )(*held)


def solution(mesh):
    placed = (
        P(("grid", "ipts"), None),
        P(("grid", "ipts"), None),
        P("ipts", "grid"),
        P("grid", "ipts"),
    )
    return jax.shard_map(
        local, mesh=mesh, in_specs=placed, out_specs=P(("grid", "ipts"), None), check_vma=False
    )
```
